32 devices in a mesh: groups: 2 (over y), blk: 4 (over z), col: 4 (over x, core).
Axes of the slice: x: 2, y: 2, z: 4, core: 2. Of those that a mesh axis runs over, the one named last changes fastest.
Arguments:
- aic: float32 [256, 32768], P(('groups', 'blk'), 'col'), parts along dimension 0, may hold values from -0.03125 to 0.03125
- downwash: float32 [8, 8192, 384], P(('groups', 'col'), 'blk'), parts along dimension 0, may hold values from -6 to 6
- node_modes: float32 [6, 32, 192], P(None, 'blk'), may hold values from -0.4375 to 0.4375
- src_rows: int32 [4, 4, 4, 8], P('blk', 'col'), may hold values from 0 to 7
- dst_nodes: int32 [4, 4, 4, 8], P('blk', 'col'), may hold values from 0 to 7
- counts: int32 [4, 4, 4], P('blk', 'col'), may hold values from 0 to 8, as said below
- spline_weights: float32 [4, 4, 6, 4, 8], P('blk', 'col'), may hold values from -0.6 to 0.6
Outputs:
- gaf: float32 [384, 384], P('groups'), parts along dimension 0
The draws below stay inside these ranges and needn't reach their ends.
There are 2 independent parts, one for each index of `groups`. The reference program is written for one: setup_inputs(seed, part) draws one part's arguments, and reference() takes and returns one part's arrays. A program takes and returns all parts, laid end to end along the dimension named above; an argument that names none is the same for every part. Nothing has to cross between parts.
Inputs may be any that keep to these rules, and one draw needn't show every extreme that they name: `counts`: slot s of a list is live when s < count; every source sub-block sends 8 live slots to its own owner, and one owner receives 8 live slots from every source sub-block. `src_rows`: rows within a sub-block of 8 rows. `dst_nodes`: nodes within an owner.
All inputs are finite; a program needn't handle non-finite values.
Results may differ from the reference program's by a relative error of at most 0.0003.
Values sent between devices are 32-bit elements; how exact they have to be, the bound alone decides.
A program may use at most 64 MiB of HBM per device.

```python
import jax
import jax.numpy as jnp
from jax import lax

PANELS = 32768
MODES = 192
ROW_DEV = 32
CAP = 8
NODE_DEV = 8
ROWS = 128
PCOL = 8192
ROW_SUB = 8
NODES = 32
N_BLK = 4
N_COL = 4


def draw_counts(key, part):
    key_level = jax.random.fold_in(key, 11)
    key_count = jax.random.fold_in(key, 12)
    key_star = jax.random.fold_in(key, 13)
    level = jax.random.randint(key_level, (N_BLK,), 0, 3)
    limit = CAP * (2 + level) // 4
    drawn = jax.random.randint(key_count, (N_BLK, N_COL, N_BLK), 0, limit[None, None, :] + 1)
    star = jax.random.randint(key_star, (), 0, N_BLK)
    owner = jnp.arange(N_BLK)[None, None, :]
    source = jnp.arange(N_BLK)[:, None, None]
    full = jnp.logical_or(owner == star, owner == source)
    return jnp.where(full, CAP, drawn).astype(jnp.int32)


def touch_ends(values, stream_key, low, high):
    shape = values.shape
    spot = [jax.random.randint(jax.random.fold_in(stream_key, axis), (), 0, shape[axis]) for axis in range(len(shape))]
    values = values.at[tuple(spot)].set(low)
    longest = shape.index(max(shape))
    spot[longest] = (spot[longest] + 1) % shape[longest]
    return values.at[tuple(spot)].set(high)


def steps_of(key, extent, split, least, top_value):
    loudness, own = 1.0, jax.random.fold_in(key, 6)
    for axis_at, shards_of in split:
        heights = jnp.exp(jax.random.uniform(jax.random.fold_in(own, axis_at), (shards_of,), jnp.float32, least / len(split), top_value / len(split)))
        loudness = loudness * jnp.repeat(heights, extent[axis_at] // shards_of).reshape([-1 if axis == axis_at else 1 for axis in range(len(extent))])
    return loudness


def gaussian(stream_key, extent, width, most, pieces=(), held_as=jnp.bfloat16):
    result = width * jax.random.normal(stream_key, extent, jnp.float32)
    if pieces:
        result = result * steps_of(stream_key, extent, pieces, -0.22, 0.18)
    return jnp.clip(result, -most, most).astype(held_as)


def setup_inputs(seed: int = 0, part: int = 0) -> dict:
    arg_keys = jax.random.split(jax.random.key(seed), 8)
    part_splits = jax.random.split(jax.random.fold_in(arg_keys[7], part), 8)
    aic = gaussian(part_splits[0], (ROWS, PANELS), PANELS ** -0.5, 0.03125, ((0, 4), (1, 4)), jnp.float32)
    downwash = gaussian(part_splits[1], (N_COL, PCOL, 2 * MODES), 1.0, 6.0, ((0, 4), (1, 4)), jnp.float32)
    node_modes = gaussian(arg_keys[2], (6, NODES, MODES), (6 * NODES) ** -0.5, 0.4375, ((1, 4),), jnp.float32)
    src_rows = touch_ends(jax.random.randint(arg_keys[3], (N_BLK, N_COL, N_BLK, CAP), 0, ROW_SUB), jax.random.fold_in(arg_keys[3], 1), 0, ROW_SUB - 1).astype(jnp.int32)
    dst_nodes = touch_ends(jax.random.randint(arg_keys[4], (N_BLK, N_COL, N_BLK, CAP), 0, NODE_DEV), jax.random.fold_in(arg_keys[4], 1), 0, NODE_DEV - 1).astype(jnp.int32)
    counts = draw_counts(jax.random.fold_in(arg_keys[7], 71), part)
    spline_weights = gaussian(arg_keys[6], (N_BLK, N_COL, 6, N_BLK, CAP), 0.1, 0.6, ((0, 4), (1, 4)), jnp.float32)
    return {"aic": aic, "downwash": downwash, "node_modes": node_modes, "src_rows": src_rows, "dst_nodes": dst_nodes, "counts": counts, "spline_weights": spline_weights}


def reference(aic, downwash, node_modes, src_rows, dst_nodes, counts, spline_weights):
    flat = downwash.reshape(PANELS, 2 * MODES)
    pressure = jnp.dot(aic, flat, precision=lax.Precision.HIGHEST, preferred_element_type=jnp.float32)
    sub_base = jnp.arange(N_COL, dtype=jnp.int32)[:, None, None] * ROW_SUB
    owner_base = jnp.arange(N_BLK, dtype=jnp.int32)[None, :, None] * NODE_DEV
    slot_index = jnp.arange(CAP, dtype=jnp.int32)[None, None, :]

    def add_block(loads, block_id):
        row_ids = (block_id * ROW_DEV + sub_base + src_rows[block_id]).astype(jnp.int32)
        node_ids = (owner_base + dst_nodes[block_id]).astype(jnp.int32)
        live = (slot_index < counts[block_id][:, :, None]).astype(jnp.float32)
        forces = pressure[row_ids]
        weights = jnp.transpose(spline_weights[block_id], (0, 2, 3, 1)) * live[..., None]
        weighted = weights[..., None] * forces[:, :, :, None, :]
        loads = loads.at[node_ids.reshape(-1)].add(weighted.reshape(-1, 6, 2 * MODES))
        return loads, None

    start = jnp.zeros((NODES, 6, 2 * MODES), jnp.float32)
    loads, unused = lax.scan(add_block, start, jnp.arange(N_BLK, dtype=jnp.int32))
    return jnp.einsum("dnm,ndk->mk", node_modes, loads, precision=lax.Precision.HIGHEST)
```

```python
import functools

import jax
import jax.numpy as jnp
from jax import lax
from jax.experimental import pallas as pl
from jax.experimental.pallas import tpu as pltpu
from jax.sharding import PartitionSpec as P


HIGHEST = lax.Precision.HIGHEST


def shifted(value, axis, steps):
    count = lax.axis_size(axis)
    pairs = [(source, (source + steps) % count) for source in range(count)]
    return lax.ppermute(value, axis, pairs)


def by_rotation(aic, downwash, node_modes, src_rows, dst_nodes, counts, spline_weights):
    cycle_size = lax.axis_size("blk")
    col_count = lax.axis_size("col")
    device = lax.axis_index("blk")
    own_block = downwash[0]
    panel_rows = own_block.shape[0]

    def product(shapes, source):
        columns = lax.dynamic_slice_in_dim(aic, source * panel_rows, panel_rows, 1)
        return jnp.dot(
            columns, shapes, precision=lax.Precision.HIGHEST, preferred_element_type=jnp.float32
        )

    halfway = cycle_size // 2

    def advance(offset, running):
        pressure, forward, behind = running
        forward = shifted(forward, "blk", 1)
        behind = shifted(behind, "blk", -1)
        pressure = pressure + product(forward, (device - offset) % cycle_size)
        pressure = pressure + product(behind, (device + offset) % cycle_size)
        return (pressure, forward, behind)

    pressure = product(own_block, device)
    pressure, forward, behind = lax.fori_loop(1, halfway, advance, (pressure, own_block, own_block))
    forward = shifted(forward, "blk", 1)
    pressure = pressure + product(forward, (device - halfway) % cycle_size)
    slots = src_rows.shape[-1]
    slot_index = jnp.arange(slots, dtype=jnp.int32)
    all_rows, all_nodes, all_counts = (
        lax.all_gather(src_rows, "col", axis=1, tiled=True),
        lax.all_gather(dst_nodes, "col", axis=1, tiled=True),
        lax.all_gather(counts, "col", axis=1, tiled=True),
    )
    weight_all = lax.all_gather(spline_weights, "col", axis=1, tiled=True)
    sub_rows = pressure.shape[0] // col_count
    offsets = jnp.arange(col_count, dtype=jnp.int32)[:, None, None] * sub_rows
    shifted_rows = all_rows[0] + offsets
    row_ids = jnp.transpose(shifted_rows, (1, 0, 2)).reshape(cycle_size, col_count * slots)
    node_ids = jnp.transpose(all_nodes[0], (1, 0, 2)).reshape(cycle_size, col_count * slots)
    live_sub = (slot_index[None, None, :] < all_counts[0][:, :, None]).astype(jnp.float32)
    live = jnp.transpose(live_sub, (1, 0, 2)).reshape(cycle_size, col_count * slots)
    weight_rows = jnp.transpose(weight_all[0], (1, 2, 0, 3)).reshape(
        6, cycle_size, col_count * slots
    )
    node_count = node_modes.shape[1]
    forces = pressure[row_ids.T]
    picks = (node_ids[None, :, :] == jnp.arange(node_count, dtype=jnp.int32)[:, None, None]).astype(
        jnp.float32
    )
    spread = weight_rows[:, None, :, :] * live[None, None, :, :] * picks[None, :, :, :]
    spread = spread.reshape(6 * node_count, cycle_size, row_ids.shape[1])
    arrived_forces, arrived_spread = (
        lax.all_to_all(forces, "blk", split_axis=1, concat_axis=1, tiled=True),
        lax.all_to_all(spread, "blk", split_axis=1, concat_axis=1, tiled=True),
    )
    loads = jnp.einsum(
        "jsc,csk->jk", arrived_spread, arrived_forces, precision=lax.Precision.HIGHEST
    )
    flat_modes = node_modes.reshape(6 * node_count, node_modes.shape[2])
    modal = jnp.einsum("jm,jk->mk", flat_modes, loads, precision=lax.Precision.HIGHEST)
    return lax.psum(modal, ("blk", "col"))


def split(value):
    high = value.astype(jnp.bfloat16)
    low = (value - high.astype(jnp.float32)).astype(jnp.bfloat16)
    return high, low


def exchange_kernel(
    blocks,
    cols,
    aic,
    panels,
    node_modes,
    rows_hbm,
    nodes_hbm,
    counts_hbm,
    weights_hbm,
    out,
    influence,
    shapes,
    shapes_high,
    shapes_low,
    partial,
    plane_in,
    line_in,
    pressure,
    spline,
    mode_rows,
    force,
    rows_list,
    nodes_list,
    counts,
    weights,
    list_sem,
    local_sem,
    aic_send,
    aic_recv,
    plane_send,
    plane_recv,
    line_send,
    line_recv,
    final_send,
    final_recv,
    spline_send,
    spline_recv,
    mode_send,
    mode_recv,
):
    b = lax.axis_index("blk")
    c = lax.axis_index("col")
    chunks, _, sub, depth = influence.shape
    dofs, _, node_count, modes = mode_rows.shape
    owners, slots = rows_list.shape[2:]
    width = panels.shape[2]
    senders = min(cols, dofs)
    while dofs % senders:
        senders -= 1
    share = dofs // senders
    pieces = local_sem.shape[0] - chunks - 1
    piece = depth // pieces

    def on_line(k):
        return lax.rem(b + k, blocks)

    def on_plane(k):
        return lax.rem(c + k, cols)

    def to_line(k, source, target, send, recv):
        return pltpu.make_async_remote_copy(
            src_ref=source,
            dst_ref=target,
            send_sem=send,
            recv_sem=recv,
            device_id={"blk": on_line(k)},
            device_id_type=pl.DeviceIdType.MESH,
        )

    def to_plane(k, source, target, send, recv):
        return pltpu.make_async_remote_copy(
            src_ref=source,
            dst_ref=target,
            send_sem=send,
            recv_sem=recv,
            device_id={"col": on_plane(k)},
            device_id_type=pl.DeviceIdType.MESH,
        )

    list_copies = []
    lists = ((rows_hbm, rows_list), (nodes_hbm, nodes_list), (counts_hbm, counts), (weights_hbm, weights))
    for i, (source, target) in enumerate(lists):
        list_copies.append(pltpu.make_async_copy(source, target, list_sem.at[i]))
        list_copies[-1].start()
    shape_copies = []
    for p in range(pieces):
        span = pl.ds(p * piece, piece)
        shape_copies.append(
            pltpu.make_async_copy(panels.at[0, span], shapes.at[span], local_sem.at[p])
        )
        shape_copies[-1].start()
    own_copies = []
    for q in range(chunks):
        own_copies.append(
            pltpu.make_async_copy(
                aic.at[pl.ds(q * sub, sub), pl.ds(pl.multiple_of(b * depth, depth), depth)],
                influence.at[q, b],
                local_sem.at[pieces + q],
            )
        )
        own_copies[-1].start()
    dof_span = pl.ds(lax.rem(c, senders) * share, share)
    own_modes = pltpu.make_async_copy(
        node_modes.at[dof_span], mode_rows.at[dof_span, b], local_sem.at[pieces + chunks]
    )

    barrier = pltpu.get_barrier_semaphore()
    for k in range(1, blocks):
        pl.semaphore_signal(
            barrier, inc=1, device_id={"blk": on_line(k)}, device_id_type=pl.DeviceIdType.MESH
        )
    for k in range(1, cols):
        pl.semaphore_signal(
            barrier, inc=1, device_id={"col": on_plane(k)}, device_id_type=pl.DeviceIdType.MESH
        )
    pl.semaphore_wait(barrier, blocks + cols - 2)

    aic_out = {}

    def send_rows(q):
        for k in range(1, blocks):
            peer = on_line(k)
            copy = to_line(
                k,
                aic.at[pl.ds(q * sub, sub), pl.ds(pl.multiple_of(peer * depth, depth), depth)],
                influence.at[q, b],
                aic_send.at[q, k - 1],
                aic_recv.at[q, k - 1],
            )
            copy.start()
            aic_out[q, k] = copy

    ahead = min(4, chunks)
    for q in range(ahead):
        send_rows(q)
        if q == 0:
            mode_out = [
                to_line(
                    k,
                    node_modes.at[dof_span],
                    mode_rows.at[dof_span, b],
                    mode_send.at[k - 1],
                    mode_recv.at[k - 1],
                )
                for k in range(1, blocks)
            ]

            @pl.when(c < senders)
            def _():
                own_modes.start()
                for copy in mode_out:
                    copy.start()

            length = dofs * owners * node_count
            row_at = lax.broadcasted_iota(jnp.int32, (sub, length), 0)
            column_at = lax.broadcasted_iota(jnp.int32, (sub, length), 1)
            total = jnp.zeros((sub, length), jnp.float32)
            for copy in list_copies:
                copy.wait()
            for o in range(owners):
                for s in range(slots):
                    live = s < counts[0, 0, o]
                    row = jnp.where(live, rows_list[0, 0, o, s], -1)
                    node = nodes_list[0, 0, o, s] + o * node_count
                    spread = jnp.zeros((sub, length), jnp.float32)
                    for d in range(dofs):
                        spread = jnp.where(
                            column_at == node + d * owners * node_count,
                            weights[0, 0, d, o, s],
                            spread,
                        )
                    total = total + jnp.where(row_at == row, spread, 0.0)
            spline[c, b] = total
            spline_out = []
            for k in range(1, blocks):
                copy = to_line(
                    k,
                    spline.at[c, b],
                    spline.at[c, b],
                    spline_send.at[k - 1],
                    spline_recv.at[k - 1],
                )
                copy.start()
                spline_out.append(copy)

    for p in range(pieces):
        shape_copies[p].wait()
        span = pl.ds(p * piece, piece)
        high, low = split(shapes[span])
        shapes_high[span] = high
        shapes_low[span] = low

    for copy in spline_out:
        copy.wait()
    for k in range(1, cols):
        copy = to_plane(
            k,
            spline.at[c],
            spline.at[c],
            spline_send.at[blocks - 2 + k],
            spline_recv.at[blocks - 2 + k],
        )
        copy.start()
        spline_out.append(copy)
    mode_plane = [
        to_plane(
            k,
            mode_rows.at[dof_span],
            mode_rows.at[dof_span],
            mode_send.at[blocks - 2 + k],
            mode_recv.at[blocks - 2 + k],
        )
        for k in range(1, cols)
    ]

    @pl.when(c < senders)
    def _():
        own_modes.wait()
        for copy in mode_out:
            copy.wait()
        for copy in mode_plane:
            copy.start()

    plane_out, line_out, final_out = {}, {}, {}

    def await_rows(q):
        own_copies[q].wait()
        for k in range(1, blocks):
            aic_out[q, k].wait_recv()

    def multiply(q):
        high, low = split(influence[q].reshape(blocks * sub, depth))
        product = jnp.dot(
            jnp.concatenate([high, low], axis=0),
            shapes_high[...],
            preferred_element_type=jnp.float32,
        )
        rest = jnp.dot(high, shapes_low[...], preferred_element_type=jnp.float32)
        lines = blocks * sub
        product = product[:lines] + (product[lines:] + rest)
        partial[q] = product.reshape(blocks, sub, width)
        for k in range(1, cols):
            copy = to_plane(
                k,
                partial.at[q, on_plane(k)],
                plane_in.at[q, k - 1],
                plane_send.at[q, k - 1],
                plane_recv.at[q, k - 1],
            )
            copy.start()
            plane_out[q, k] = copy

    def over_plane(q):
        total = partial[q, c]
        for k in range(1, cols):
            plane_out[q, k].wait_recv()
            total = total + plane_in[q, k - 1]
        line_in[q, b] = total
        for k in range(1, blocks):
            copy = to_line(
                k,
                line_in.at[q, b],
                line_in.at[q, b],
                line_send.at[q, k - 1],
                line_recv.at[q, k - 1],
            )
            copy.start()
            line_out[q, k] = copy

    def over_line(q):
        for k in range(1, blocks):
            line_out[q, k].wait_recv()
        total = line_in[q, 0]
        for source in range(1, blocks):
            total = total + line_in[q, source]
        pressure[q, c] = total
        for k in range(1, cols):
            copy = to_plane(
                k,
                pressure.at[q, c],
                pressure.at[q, c],
                final_send.at[q, k - 1],
                final_recv.at[q, k - 1],
            )
            copy.start()
            final_out[q, k] = copy

    def make_force():
        for k in range(1, cols):
            spline_out[blocks - 2 + k].wait_recv()

            @pl.when(lax.rem(c + cols - k, cols) < senders)
            def _():
                mode_plane[k - 1].wait_recv()

        length = dofs * owners * node_count
        force[...] = jnp.dot(
            spline[...].reshape(cols * blocks * sub, length),
            mode_rows[...].reshape(length, modes),
            precision=HIGHEST,
            preferred_element_type=jnp.float32,
        )

    def modal(start, stop):
        force_rows = force[pl.ds(start * blocks * sub, (stop - start) * blocks * sub)]
        return lax.dot_general(
            force_rows,
            pressure[start:stop].reshape((stop - start) * blocks * sub, width),
            (((0,), (0,)), ((), ())),
            precision=HIGHEST,
            preferred_element_type=jnp.float32,
        )

    def await_pressure(q):
        for k in range(1, cols):
            final_out[q, k].wait_recv()

    for q in range(chunks):
        await_rows(q)
        if q + ahead < chunks:
            send_rows(q + ahead)
        multiply(q)
        if q == chunks - 1:
            for earlier in range(q):
                over_plane(earlier)
        if q == 1:
            make_force()
    last = chunks - 1
    over_plane(last)
    for q in range(chunks):
        over_line(q)
    if last:
        for q in range(last):
            await_pressure(q)
        out[...] = modal(0, last)
        await_pressure(last)
        out[...] += modal(last, chunks)
    else:
        await_pressure(last)
        out[...] = modal(last, chunks)

    for copy in spline_out[blocks - 1 :]:
        copy.wait_send()
    for group in (aic_out, plane_out, line_out, final_out):
        for copy in group.values():
            copy.wait_send()

    @pl.when(c < senders)
    def _():
        for copy in mode_plane:
            copy.wait_send()


def by_kernel(aic, downwash, node_modes, src_rows, dst_nodes, counts, spline_weights):
    blocks = lax.axis_size("blk")
    cols = lax.axis_size("col")
    rows = aic.shape[0]
    sub = rows // cols
    depth, width = downwash.shape[1:]
    dofs, node_count, modes = node_modes.shape
    length = dofs * blocks * node_count
    pieces = 4
    dma = pltpu.SemaphoreType.DMA
    anywhere = pl.BlockSpec(memory_space=pl.ANY)
    operands = (aic, downwash, node_modes, src_rows, dst_nodes, counts, spline_weights)
    in_hbm = [pltpu.with_memory_space_constraint(v, pltpu.MemorySpace.HBM) for v in operands]
    return pl.pallas_call(
        functools.partial(exchange_kernel, blocks, cols),
        name="gaf_exchange",
        out_shape=jax.ShapeDtypeStruct((modes, width), jnp.float32),
        in_specs=[anywhere] * 7,
        out_specs=pl.BlockSpec(memory_space=pltpu.VMEM),
        scratch_shapes=[
            pltpu.VMEM((cols, blocks, sub, depth), jnp.float32),
            pltpu.VMEM((depth, width), jnp.float32),
            pltpu.VMEM((depth, width), jnp.bfloat16),
            pltpu.VMEM((depth, width), jnp.bfloat16),
            pltpu.VMEM((cols, blocks, sub, width), jnp.float32),
            pltpu.VMEM((cols, cols - 1, sub, width), jnp.float32),
            pltpu.VMEM((cols, blocks, sub, width), jnp.float32),
            pltpu.VMEM((cols, blocks, sub, width), jnp.float32),
            pltpu.VMEM((cols, blocks, sub, length), jnp.float32),
            pltpu.VMEM((dofs, blocks, node_count, modes), jnp.float32),
            pltpu.VMEM((cols * blocks * sub, modes), jnp.float32),
            pltpu.SMEM(src_rows.shape, jnp.int32),
            pltpu.SMEM(dst_nodes.shape, jnp.int32),
            pltpu.SMEM(counts.shape, jnp.int32),
            pltpu.SMEM(spline_weights.shape, jnp.float32),
            dma((4,)),
            dma((pieces + cols + 1,)),
            dma((cols, blocks - 1)),
            dma((cols, blocks - 1)),
            dma((cols, cols - 1)),
            dma((cols, cols - 1)),
            dma((cols, blocks - 1)),
            dma((cols, blocks - 1)),
            dma((cols, cols - 1)),
            dma((cols, cols - 1)),
            dma((blocks + cols - 2,)),
            dma((blocks + cols - 2,)),
            dma((blocks + cols - 2,)),
            dma((blocks + cols - 2,)),
        ],
        compiler_params=pltpu.CompilerParams(
            collective_id=0, has_side_effects=True, vmem_limit_bytes=32 * 1024 * 1024
        ),
    )(*in_hbm)


def solution(mesh):
    placed = (
        P(("groups", "blk"), "col"),
        P(("groups", "col"), "blk", None),
        P(None, "blk", None),
        P("blk", "col", None, None),
        P("blk", "col", None, None),
        P("blk", "col", None),
        P("blk", "col", None, None, None),
    )

    def shards(*operands):
        aic, downwash, node_modes = operands[:3]
        blocks, cols = lax.axis_size("blk"), lax.axis_size("col")
        small = blocks * aic.shape[0] <= 2 * node_modes.shape[2]
        even = blocks == cols and aic.shape[0] % (8 * cols) == 0 and downwash.shape[1] % 512 == 0
        if small and even:
            return by_kernel(*operands)
        return by_rotation(*operands)

    return jax.shard_map(
        shards, mesh=mesh, in_specs=placed, out_specs=P("groups", None), check_vma=False
    )
```

```python
import functools

import jax
import jax.numpy as jnp
from jax import lax
from jax.experimental import pallas as pl
from jax.experimental.pallas import tpu as pltpu
from jax.sharding import PartitionSpec as P


HIGHEST = lax.Precision.HIGHEST
PARTS = 2
AHEAD = 4
OWNED = (0,)
LISTS_AT = 3
SPREAD_AT = 7
ODD_AHEAD = 2


def shifted(value, axis, steps):
    count = lax.axis_size(axis)
    pairs = [(source, (source + steps) % count) for source in range(count)]
    return lax.ppermute(value, axis, pairs)


def by_rotation(aic, downwash, node_modes, src_rows, dst_nodes, counts, spline_weights):
    cycle_size = lax.axis_size("blk")
    col_count = lax.axis_size("col")
    device = lax.axis_index("blk")
    own_block = downwash[0]
    panel_rows = own_block.shape[0]

    def product(shapes, source):
        columns = lax.dynamic_slice_in_dim(aic, source * panel_rows, panel_rows, 1)
        return jnp.dot(
            columns, shapes, precision=lax.Precision.HIGHEST, preferred_element_type=jnp.float32
        )

    halfway = cycle_size // 2

    def advance(offset, running):
        pressure, forward, behind = running
        forward = shifted(forward, "blk", 1)
        behind = shifted(behind, "blk", -1)
        pressure = pressure + product(forward, (device - offset) % cycle_size)
        pressure = pressure + product(behind, (device + offset) % cycle_size)
        return (pressure, forward, behind)

    pressure = product(own_block, device)
    pressure, forward, behind = lax.fori_loop(1, halfway, advance, (pressure, own_block, own_block))
    forward = shifted(forward, "blk", 1)
    pressure = pressure + product(forward, (device - halfway) % cycle_size)
    slots = src_rows.shape[-1]
    slot_index = jnp.arange(slots, dtype=jnp.int32)
    all_rows, all_nodes, all_counts = (
        lax.all_gather(src_rows, "col", axis=1, tiled=True),
        lax.all_gather(dst_nodes, "col", axis=1, tiled=True),
        lax.all_gather(counts, "col", axis=1, tiled=True),
    )
    weight_all = lax.all_gather(spline_weights, "col", axis=1, tiled=True)
    sub_rows = pressure.shape[0] // col_count
    offsets = jnp.arange(col_count, dtype=jnp.int32)[:, None, None] * sub_rows
    shifted_rows = all_rows[0] + offsets
    row_ids = jnp.transpose(shifted_rows, (1, 0, 2)).reshape(cycle_size, col_count * slots)
    node_ids = jnp.transpose(all_nodes[0], (1, 0, 2)).reshape(cycle_size, col_count * slots)
    live_sub = (slot_index[None, None, :] < all_counts[0][:, :, None]).astype(jnp.float32)
    live = jnp.transpose(live_sub, (1, 0, 2)).reshape(cycle_size, col_count * slots)
    weight_rows = jnp.transpose(weight_all[0], (1, 2, 0, 3)).reshape(
        6, cycle_size, col_count * slots
    )
    node_count = node_modes.shape[1]
    forces = pressure[row_ids.T]
    picks = (node_ids[None, :, :] == jnp.arange(node_count, dtype=jnp.int32)[:, None, None]).astype(
        jnp.float32
    )
    spread = weight_rows[:, None, :, :] * live[None, None, :, :] * picks[None, :, :, :]
    spread = spread.reshape(6 * node_count, cycle_size, row_ids.shape[1])
    arrived_forces, arrived_spread = (
        lax.all_to_all(forces, "blk", split_axis=1, concat_axis=1, tiled=True),
        lax.all_to_all(spread, "blk", split_axis=1, concat_axis=1, tiled=True),
    )
    loads = jnp.einsum(
        "jsc,csk->jk", arrived_spread, arrived_forces, precision=lax.Precision.HIGHEST
    )
    flat_modes = node_modes.reshape(6 * node_count, node_modes.shape[2])
    modal = jnp.einsum("jm,jk->mk", flat_modes, loads, precision=lax.Precision.HIGHEST)
    return lax.psum(modal, ("blk", "col"))


def split(value):
    high = value.astype(jnp.bfloat16)
    low = (value - high.astype(jnp.float32)).astype(jnp.bfloat16)
    return high, low


def exchange_kernel(
    blocks,
    cols,
    aic,
    panels,
    node_modes,
    rows_hbm,
    nodes_hbm,
    counts_hbm,
    weights_hbm,
    out,
    influence,
    shapes,
    shapes_high,
    shapes_low,
    partial,
    plane_in,
    line_in,
    gather_in,
    pressure,
    spline,
    mode_rows,
    force,
    rows_list,
    nodes_list,
    counts,
    weights,
    list_sem,
    panel_sem,
    aic_recv,
    aic_send,
    plane_recv,
    plane_send,
    line_recv,
    line_send,
    back_recv,
    final_recv,
    final_send,
    gather_recv,
    gather_send,
    cast_recv,
    cast_send,
    spline_recv,
    spline_send,
    mode_recv,
    mode_send,
    mode_plane_recv,
):
    b = lax.axis_index("blk")
    c = lax.axis_index("col")
    chunks, _, sub, depth = influence.shape
    dofs, _, node_count, modes = mode_rows.shape
    owners, slots = rows_list.shape[2:]
    width = panels.shape[2]
    last = chunks - 1
    early = range(last)
    parts = PARTS
    span = depth // parts
    total_pieces = chunks * parts
    middle = blocks // 2
    length = dofs * owners * node_count

    def on_line(k):
        return lax.rem(b + k, blocks)

    def on_plane(k):
        return lax.rem(c + k, cols)

    def far_target(j):
        falling = blocks - 1 - j
        rising = j
        falling = jnp.where(falling <= b, falling - 1, falling)
        rising = jnp.where(rising >= b, rising + 1, rising)
        return jnp.where(b < middle, falling, rising)

    def remote(where, source, target, send, recv):
        return pltpu.make_async_remote_copy(
            src_ref=source,
            dst_ref=target,
            send_sem=send,
            recv_sem=recv,
            device_id=where,
            device_id_type=pl.DeviceIdType.MESH,
        )

    def settle(ref, sem):
        pltpu.make_async_copy(ref, ref, sem).wait()

    barrier = pltpu.get_barrier_semaphore()
    for z in range(blocks):
        for x in range(cols):
            if (z == 0) != (x == 0):
                pl.semaphore_signal(
                    barrier,
                    inc=1,
                    device_id={"blk": on_line(z), "col": on_plane(x)},
                    device_id_type=pl.DeviceIdType.MESH,
                )

    list_copies = []
    lists = ((rows_hbm, rows_list), (nodes_hbm, nodes_list), (counts_hbm, counts), (weights_hbm, weights))
    for i, (source, target) in enumerate(lists):
        list_copies.append(pltpu.make_async_copy(source, target, list_sem.at[i]))
        list_copies[-1].start()
    stripes = panel_sem.shape[0] - 1
    stripe = depth // stripes
    panel_copies = []
    for p in range(stripes):
        where = pl.ds(p * stripe, stripe)
        panel_copies.append(
            pltpu.make_async_copy(panels.at[0, where], shapes.at[where], panel_sem.at[p])
        )
        panel_copies[-1].start()

    def piece_of(index):
        q, h = divmod(index, parts)
        return q, pl.ds(h * span, span)

    def aic_piece(index, peer):
        q, h = divmod(index, parts)
        start = pl.multiple_of(peer * depth + h * span, 128)
        return aic.at[pl.ds(q * sub, sub), pl.ds(start, span)]

    for index in range(total_pieces):
        q, where = piece_of(index)
        pltpu.make_async_copy(
            aic_piece(index, b), influence.at[q, b, :, where], aic_recv.at[index]
        ).start()
    half = cols // 2
    share = dofs // 2
    dof_span = pl.ds((c // half) * share, share)
    sends_modes = lax.rem(c, half) == 0
    own_modes = pltpu.make_async_copy(
        node_modes.at[dof_span], mode_rows.at[dof_span, b], panel_sem.at[stripes]
    )

    @pl.when(sends_modes)
    def _():
        own_modes.start()

    pl.semaphore_wait(barrier, blocks + cols - 2)

    def send_piece(index, parity):
        if index >= total_pieces:
            return
        q, where = piece_of(index)

        @pl.when(lax.rem(c, 2) == parity)
        def _():
            for j in range(blocks - 1):
                peer = far_target(j)
                remote(
                    {"blk": peer},
                    aic_piece(index, peer),
                    influence.at[q, b, :, where],
                    aic_send,
                    aic_recv.at[index],
                ).start()

    def await_piece(index):
        q, where = piece_of(index)
        settle(influence.at[q, :, :, where], aic_recv.at[index])
        send_piece(index + AHEAD, 0)
        send_piece(index + ODD_AHEAD, 1)

    for index in range(max(AHEAD, ODD_AHEAD)):
        if index < AHEAD:
            send_piece(index, 0)
        if index < ODD_AHEAD:
            send_piece(index, 1)

    row_at = lax.broadcasted_iota(jnp.int32, (sub, length), 0)
    column_at = lax.broadcasted_iota(jnp.int32, (sub, length), 1)
    total = jnp.zeros((sub, length), jnp.float32)
    for copy in list_copies:
        copy.wait()
    for o in range(owners):
        for s in range(slots):
            live = s < counts[0, 0, o]
            row = jnp.where(live, rows_list[0, 0, o, s], -1)
            node = nodes_list[0, 0, o, s] + o * node_count
            spread = jnp.zeros((sub, length), jnp.float32)
            for d in range(dofs):
                spread = jnp.where(
                    column_at == node + d * owners * node_count,
                    weights[0, 0, d, o, s],
                    spread,
                )
            total = total + jnp.where(row_at == row, spread, 0.0)
    spline[c, b] = total

    for p in range(stripes):
        panel_copies[p].wait()
        where = pl.ds(p * stripe, stripe)
        high, low = split(shapes[where])
        shapes_high[where] = high
        shapes_low[where] = low

    def multiply(q, start, stop):
        where = pl.ds(start * span, (stop - start) * span)
        lines = blocks * sub
        high, low = split(influence[q, :, :, where].reshape(lines, (stop - start) * span))
        product = jnp.dot(
            jnp.concatenate([high, low], axis=0),
            shapes_high[where],
            preferred_element_type=jnp.float32,
        )
        rest = jnp.dot(high, shapes_low[where], preferred_element_type=jnp.float32)
        return product[:lines] + (product[lines:] + rest)

    def to_plane(q):
        partial[q] = multiply(q, 0, parts).reshape(blocks, sub, width)
        for k in range(1, cols):
            remote(
                {"col": on_plane(k)},
                partial.at[q, on_plane(k)],
                plane_in.at[q, k - 1],
                plane_send,
                plane_recv.at[q],
            ).start()

    def keeper(q):
        return middle - 1 + q % 2 if q in OWNED else None

    def over_plane(q):
        settle(plane_in.at[q], plane_recv.at[q])
        total = partial[q, c]
        for k in range(1, cols):
            total = total + plane_in[q, k - 1]
        line_in[q, b] = total
        keep = keeper(q)
        if keep is None:
            for j in range(blocks - 1):
                remote(
                    {"blk": far_target(j)},
                    line_in.at[q, b],
                    line_in.at[q, b],
                    line_send.at[q],
                    line_recv.at[q],
                ).start()
        else:

            @pl.when(b != keep)
            def _():
                remote(
                    {"blk": keep},
                    line_in.at[q, b],
                    line_in.at[q, b],
                    line_send.at[q],
                    line_recv.at[q],
                ).start()

    def sum_line(q):
        settle(line_in.at[q, pl.ds(0, blocks - 1)], line_recv.at[q])
        total = line_in[q, 0]
        for source in range(1, blocks):
            total = total + line_in[q, source]
        pressure[q, c] = total

    def to_final(q):
        for k in range(1, cols):
            remote(
                {"col": on_plane(k)},
                pressure.at[q, c],
                pressure.at[q, c],
                final_send,
                final_recv.at[q],
            ).start()

    def keep_line(q):
        keep = keeper(q)
        if keep is None:
            return

        @pl.when(b == keep)
        def _():
            sum_line(q)
            for j in range(blocks - 1):
                remote(
                    {"blk": far_target(j)},
                    pressure.at[q, c],
                    pressure.at[q, c],
                    line_send.at[q],
                    back_recv.at[q],
                ).start()
            to_final(q)

    def finish_line(q):
        keep = keeper(q)
        if keep is None:
            sum_line(q)
            to_final(q)
        else:

            @pl.when(b != keep)
            def _():
                settle(pressure.at[q, c], back_recv.at[q])
                to_final(q)

    def seat(r):
        return middle - 1 + r % 2

    is_owner = b == middle - 1 + lax.rem(c, 2)

    def to_owners():
        for r in range(cols):

            @pl.when(jnp.logical_or(b != seat(r), c != r))
            def _():
                remote(
                    {"blk": seat(r), "col": r},
                    partial.at[last, r],
                    gather_in.at[b * cols + c],
                    gather_send,
                    gather_recv,
                ).start()

    def cast():
        @pl.when(is_owner)
        def _():
            gather_in[b * cols + c] = partial[last, c]
            settle(gather_in.at[pl.ds(0, blocks * cols - 1)], gather_recv)
            total = gather_in[0]
            for source in range(1, blocks * cols):
                total = total + gather_in[source]
            pressure[last, c] = total
            for j in range(blocks):
                for k in range(cols):
                    if j == blocks - 1 and k == 0:
                        continue
                    peer = b if j == blocks - 1 else far_target(j)
                    remote(
                        {"blk": peer, "col": on_plane(k)},
                        pressure.at[last, c],
                        pressure.at[last, c],
                        cast_send,
                        cast_recv,
                    ).start()

    def await_cast():
        @pl.when(is_owner)
        def _():
            settle(pressure.at[last, pl.ds(0, cols - 1)], cast_recv)

        @pl.when(jnp.logical_not(is_owner))
        def _():
            settle(pressure.at[last], cast_recv)

    def spline_to_line():
        for j in range(blocks - 1):
            remote(
                {"blk": far_target(j)},
                spline.at[c, b],
                spline.at[c, b],
                spline_send.at[0],
                spline_recv.at[0],
            ).start()

        @pl.when(sends_modes)
        def _():
            for j in range(blocks - 1):
                remote(
                    {"blk": far_target(j)},
                    node_modes.at[dof_span],
                    mode_rows.at[dof_span, b],
                    mode_send.at[0],
                    mode_recv,
                ).start()

    def spline_to_plane():
        settle(spline.at[c, pl.ds(0, blocks - 1)], spline_recv.at[0])
        for k in range(1, cols):
            remote(
                {"col": on_plane(k)},
                spline.at[c],
                spline.at[c],
                spline_send.at[1],
                spline_recv.at[1],
            ).start()

        @pl.when(sends_modes)
        def _():
            own_modes.wait()
            settle(mode_rows.at[dof_span, pl.ds(0, blocks - 1)], mode_recv)
            for k in range(1, cols):
                remote(
                    {"col": on_plane(k)},
                    mode_rows.at[dof_span],
                    mode_rows.at[dof_span],
                    mode_send.at[k],
                    mode_plane_recv.at[c // half],
                ).start()

    def make_force():
        settle(spline.at[pl.ds(0, cols - 1)], spline_recv.at[1])
        for s in range(2):

            @pl.when(c != s * half)
            def _():
                settle(mode_rows.at[pl.ds(s * share, share)], mode_plane_recv.at[s])

        force[...] = jnp.dot(
            spline[...].reshape(cols * blocks * sub, length),
            mode_rows[...].reshape(length, modes),
            precision=HIGHEST,
            preferred_element_type=jnp.float32,
        )

    def modal(start, stop):
        force_rows = force[pl.ds(start * blocks * sub, (stop - start) * blocks * sub)]
        return lax.dot_general(
            force_rows,
            pressure[start:stop].reshape((stop - start) * blocks * sub, width),
            (((0,), (0,)), ((), ())),
            precision=HIGHEST,
            preferred_element_type=jnp.float32,
        )

    for index in range(total_pieces):
        await_piece(index)
        if index == LISTS_AT:
            spline_to_line()
        q, h = divmod(index, parts)
        if q == last:
            product = multiply(last, h, h + 1)
            ending = product if h == 0 else ending + product
            if h == 0:
                keep_line(0)
        elif h == parts - 1:
            to_plane(q)
            if q > 0:
                over_plane(q - 1)
        if index == SPREAD_AT and index < total_pieces - 1:
            spline_to_plane()
    partial[last] = ending.reshape(blocks, sub, width)
    to_owners()
    if SPREAD_AT >= total_pieces - 1:
        spline_to_plane()
    over_plane(last - 1)
    finish_line(0)
    cast()
    for q in range(1, last):
        finish_line(q)
    make_force()
    for q in early:
        settle(pressure.at[q, pl.ds(0, cols - 1)], final_recv.at[q])
    out[...] = modal(0, last)
    await_cast()
    out[...] += modal(last, chunks)

    settle(influence.at[pl.ds(0, blocks - 1)], aic_send)
    settle(plane_in, plane_send)
    settle(plane_in, final_send)
    settle(spline.at[c, pl.ds(0, blocks - 1)], spline_send.at[0])
    settle(spline.at[pl.ds(0, cols - 1)], spline_send.at[1])
    for q in early:
        keep = keeper(q)
        if keep is None:
            settle(line_in.at[q, pl.ds(0, blocks - 1)], line_send.at[q])
        else:

            @pl.when(b == keep)
            def _():
                settle(line_in.at[q, pl.ds(0, blocks - 1)], line_send.at[q])

            @pl.when(b != keep)
            def _():
                settle(line_in.at[q, 0], line_send.at[q])

    @pl.when(is_owner)
    def _():
        settle(partial.at[last, pl.ds(0, cols - 1)], gather_send)
        settle(gather_in.at[pl.ds(0, blocks * cols - 1)], cast_send)

    @pl.when(jnp.logical_not(is_owner))
    def _():
        settle(partial.at[last], gather_send)

    @pl.when(sends_modes)
    def _():
        settle(mode_rows.at[dof_span, pl.ds(0, blocks - 1)], mode_send.at[0])
        settle(mode_rows.at[dof_span], mode_send.at[1])
        for k in range(2, cols):
            settle(mode_rows.at[dof_span], mode_send.at[k])


def by_kernel(aic, downwash, node_modes, src_rows, dst_nodes, counts, spline_weights):
    blocks = lax.axis_size("blk")
    cols = lax.axis_size("col")
    rows = aic.shape[0]
    sub = rows // cols
    depth, width = downwash.shape[1:]
    dofs, node_count, modes = node_modes.shape
    length = dofs * blocks * node_count
    stripes = 4
    dma = pltpu.SemaphoreType.DMA
    anywhere = pl.BlockSpec(memory_space=pl.ANY)
    operands = (aic, downwash, node_modes, src_rows, dst_nodes, counts, spline_weights)
    in_hbm = [pltpu.with_memory_space_constraint(v, pltpu.MemorySpace.HBM) for v in operands]
    return pl.pallas_call(
        functools.partial(exchange_kernel, blocks, cols),
        name="gaf_exchange",
        out_shape=jax.ShapeDtypeStruct((modes, width), jnp.float32),
        in_specs=[anywhere] * 7,
        out_specs=pl.BlockSpec(memory_space=pltpu.VMEM),
        scratch_shapes=[
            pltpu.VMEM((cols, blocks, sub, depth), jnp.float32),
            pltpu.VMEM((depth, width), jnp.float32),
            pltpu.VMEM((depth, width), jnp.bfloat16),
            pltpu.VMEM((depth, width), jnp.bfloat16),
            pltpu.VMEM((cols, blocks, sub, width), jnp.float32),
            pltpu.VMEM((cols - 1, cols - 1, sub, width), jnp.float32),
            pltpu.VMEM((cols - 1, blocks, sub, width), jnp.float32),
            pltpu.VMEM((blocks * cols, sub, width), jnp.float32),
            pltpu.VMEM((cols, blocks, sub, width), jnp.float32),
            pltpu.VMEM((cols, blocks, sub, length), jnp.float32),
            pltpu.VMEM((dofs, blocks, node_count, modes), jnp.float32),
            pltpu.VMEM((cols * blocks * sub, modes), jnp.float32),
            pltpu.SMEM(src_rows.shape, jnp.int32),
            pltpu.SMEM(dst_nodes.shape, jnp.int32),
            pltpu.SMEM(counts.shape, jnp.int32),
            pltpu.SMEM(spline_weights.shape, jnp.float32),
            dma((4,)),
            dma((stripes + 1,)),
            dma((cols * PARTS,)),
            dma,
            dma((cols - 1,)),
            dma,
            dma((cols - 1,)),
            dma((cols - 1,)),
            dma((cols - 1,)),
            dma((cols - 1,)),
            dma,
            dma,
            dma,
            dma,
            dma,
            dma((2,)),
            dma((2,)),
            dma,
            dma((cols,)),
            dma((2,)),
        ],
        compiler_params=pltpu.CompilerParams(
            collective_id=0, has_side_effects=True, vmem_limit_bytes=32 * 1024 * 1024
        ),
    )(*in_hbm)


def solution(mesh):
    placed = (
        P(("groups", "blk"), "col"),
        P(("groups", "col"), "blk", None),
        P(None, "blk", None),
        P("blk", "col", None, None),
        P("blk", "col", None, None),
        P("blk", "col", None),
        P("blk", "col", None, None, None),
    )

    def shards(*operands):
        aic, downwash, node_modes = operands[:3]
        blocks, cols = lax.axis_size("blk"), lax.axis_size("col")
        small = blocks * aic.shape[0] <= 2 * node_modes.shape[2]
        even = blocks == cols and cols % 2 == 0 and node_modes.shape[0] % 2 == 0 and aic.shape[0] % (8 * cols) == 0 and downwash.shape[1] % 512 == 0
        if small and even:
            return by_kernel(*operands)
        return by_rotation(*operands)

    return jax.shard_map(
        shards, mesh=mesh, in_specs=placed, out_specs=P("groups", None), check_vma=False
    )
```

```python
import functools

import jax
import jax.numpy as jnp
from jax import lax
from jax.experimental import pallas as pl
from jax.experimental.pallas import tpu as pltpu
from jax.sharding import PartitionSpec as P


HIGHEST = lax.Precision.HIGHEST
PARTS = 2
AHEAD = 3
SECOND_AT = 1
THIRD_AT = 4
OPENING = 2
LAST_AT = None
AFTER = {4: ((0, 0),), 6: ((0, 1),)}
TAIL = ((0, 2), (1, 0), (1, 1), (1, 2))
FINAL = ()
ODD_AHEAD = 2


def shifted(value, axis, steps):
    count = lax.axis_size(axis)
    pairs = [(source, (source + steps) % count) for source in range(count)]
    return lax.ppermute(value, axis, pairs)


def by_rotation(aic, downwash, node_modes, src_rows, dst_nodes, counts, spline_weights):
    cycle_size = lax.axis_size("blk")
    col_count = lax.axis_size("col")
    device = lax.axis_index("blk")
    own_block = downwash[0]
    panel_rows = own_block.shape[0]

    def product(shapes, source):
        columns = lax.dynamic_slice_in_dim(aic, source * panel_rows, panel_rows, 1)
        return jnp.dot(
            columns, shapes, precision=lax.Precision.HIGHEST, preferred_element_type=jnp.float32
        )

    halfway = cycle_size // 2

    def advance(offset, running):
        pressure, forward, behind = running
        forward = shifted(forward, "blk", 1)
        behind = shifted(behind, "blk", -1)
        pressure = pressure + product(forward, (device - offset) % cycle_size)
        pressure = pressure + product(behind, (device + offset) % cycle_size)
        return (pressure, forward, behind)

    pressure = product(own_block, device)
    pressure, forward, behind = lax.fori_loop(1, halfway, advance, (pressure, own_block, own_block))
    forward = shifted(forward, "blk", 1)
    pressure = pressure + product(forward, (device - halfway) % cycle_size)
    slots = src_rows.shape[-1]
    slot_index = jnp.arange(slots, dtype=jnp.int32)
    all_rows, all_nodes, all_counts = (
        lax.all_gather(src_rows, "col", axis=1, tiled=True),
        lax.all_gather(dst_nodes, "col", axis=1, tiled=True),
        lax.all_gather(counts, "col", axis=1, tiled=True),
    )
    weight_all = lax.all_gather(spline_weights, "col", axis=1, tiled=True)
    sub_rows = pressure.shape[0] // col_count
    offsets = jnp.arange(col_count, dtype=jnp.int32)[:, None, None] * sub_rows
    shifted_rows = all_rows[0] + offsets
    row_ids = jnp.transpose(shifted_rows, (1, 0, 2)).reshape(cycle_size, col_count * slots)
    node_ids = jnp.transpose(all_nodes[0], (1, 0, 2)).reshape(cycle_size, col_count * slots)
    live_sub = (slot_index[None, None, :] < all_counts[0][:, :, None]).astype(jnp.float32)
    live = jnp.transpose(live_sub, (1, 0, 2)).reshape(cycle_size, col_count * slots)
    weight_rows = jnp.transpose(weight_all[0], (1, 2, 0, 3)).reshape(
        6, cycle_size, col_count * slots
    )
    node_count = node_modes.shape[1]
    forces = pressure[row_ids.T]
    picks = (node_ids[None, :, :] == jnp.arange(node_count, dtype=jnp.int32)[:, None, None]).astype(
        jnp.float32
    )
    spread = weight_rows[:, None, :, :] * live[None, None, :, :] * picks[None, :, :, :]
    spread = spread.reshape(6 * node_count, cycle_size, row_ids.shape[1])
    arrived_forces, arrived_spread = (
        lax.all_to_all(forces, "blk", split_axis=1, concat_axis=1, tiled=True),
        lax.all_to_all(spread, "blk", split_axis=1, concat_axis=1, tiled=True),
    )
    loads = jnp.einsum(
        "jsc,csk->jk", arrived_spread, arrived_forces, precision=lax.Precision.HIGHEST
    )
    flat_modes = node_modes.reshape(6 * node_count, node_modes.shape[2])
    modal = jnp.einsum("jm,jk->mk", flat_modes, loads, precision=lax.Precision.HIGHEST)
    return lax.psum(modal, ("blk", "col"))


def split(value):
    high = value.astype(jnp.bfloat16)
    low = (value - high.astype(jnp.float32)).astype(jnp.bfloat16)
    return high, low


def exchange_kernel(
    blocks,
    cols,
    aic,
    panels,
    node_modes,
    rows_hbm,
    nodes_hbm,
    counts_hbm,
    weights_hbm,
    out,
    influence,
    shapes,
    shapes_high,
    shapes_low,
    partial,
    half_in,
    half_out,
    cross_in,
    gather_in,
    pressure,
    spline,
    mode_rows,
    force,
    rows_list,
    nodes_list,
    counts,
    weights,
    list_sem,
    panel_sem,
    aic_recv,
    aic_send,
    half_recv,
    half_send,
    cross_recv,
    cross_send,
    final_recv,
    final_send,
    gather_recv,
    gather_send,
    cast_recv,
    cast_send,
    chain_recv,
    chain_send,
    spline_recv,
    spline_send,
    mode_recv,
    mode_send,
    mode_plane_recv,
):
    b = lax.axis_index("blk")
    c = lax.axis_index("col")
    chunks, _, sub, depth = influence.shape
    dofs, _, node_count, modes = mode_rows.shape
    owners, slots = rows_list.shape[2:]
    width = panels.shape[2]
    last = chunks - 1
    early = range(last)
    parts = PARTS
    span = depth // parts
    total_pieces = chunks * parts
    middle = blocks // 2
    length = dofs * owners * node_count

    def on_line(k):
        return lax.rem(b + k, blocks)

    def on_plane(k):
        return lax.rem(c + k, cols)

    def far_target(j):
        falling = blocks - 1 - j
        rising = j
        falling = jnp.where(falling <= b, falling - 1, falling)
        rising = jnp.where(rising >= b, rising + 1, rising)
        return jnp.where(b < middle, falling, rising)

    def remote(where, source, target, send, recv):
        return pltpu.make_async_remote_copy(
            src_ref=source,
            dst_ref=target,
            send_sem=send,
            recv_sem=recv,
            device_id=where,
            device_id_type=pl.DeviceIdType.MESH,
        )

    def settle(ref, sem):
        pltpu.make_async_copy(ref, ref, sem).wait()

    barrier = pltpu.get_barrier_semaphore()
    for z in range(blocks):
        for x in range(cols):
            if (z == 0) != (x == 0):
                pl.semaphore_signal(
                    barrier,
                    inc=1,
                    device_id={"blk": on_line(z), "col": on_plane(x)},
                    device_id_type=pl.DeviceIdType.MESH,
                )

    list_copies = []
    lists = ((rows_hbm, rows_list), (nodes_hbm, nodes_list), (counts_hbm, counts), (weights_hbm, weights))
    for i, (source, target) in enumerate(lists):
        list_copies.append(pltpu.make_async_copy(source, target, list_sem.at[i]))
        list_copies[-1].start()
    stripes = panel_sem.shape[0] - 1
    stripe = depth // stripes
    panel_copies = []
    for p in range(stripes):
        where = pl.ds(p * stripe, stripe)
        panel_copies.append(
            pltpu.make_async_copy(panels.at[0, where], shapes.at[where], panel_sem.at[p])
        )
        panel_copies[-1].start()

    def piece_of(index):
        q, h = divmod(index, parts)
        return q, pl.ds(h * span, span)

    def aic_piece(index, peer):
        q, h = divmod(index, parts)
        start = pl.multiple_of(peer * depth + h * span, 128)
        return aic.at[pl.ds(q * sub, sub), pl.ds(start, span)]

    for index in range(total_pieces):
        q, where = piece_of(index)
        pltpu.make_async_copy(
            aic_piece(index, b), influence.at[q, b, :, where], aic_recv.at[index]
        ).start()
    half = cols // 2
    share = dofs // 2
    dof_span = pl.ds((c // half) * share, share)
    sends_modes = lax.rem(c, half) == half - 1
    own_modes = pltpu.make_async_copy(
        node_modes.at[dof_span], mode_rows.at[dof_span, b], panel_sem.at[stripes]
    )

    @pl.when(sends_modes)
    def _():
        own_modes.start()

    pl.semaphore_wait(barrier, blocks + cols - 2)

    def send_piece(index, parity):
        if index >= total_pieces:
            return
        q, where = piece_of(index)

        @pl.when(lax.rem(c, 2) == parity)
        def _():
            for j in range(blocks - 1):
                peer = far_target(j)
                remote(
                    {"blk": peer},
                    aic_piece(index, peer),
                    influence.at[q, b, :, where],
                    aic_send,
                    aic_recv.at[index],
                ).start()

    def await_piece(index):
        q, where = piece_of(index)
        settle(influence.at[q, :, :, where], aic_recv.at[index])
        send_piece(index + AHEAD, 0)
        send_piece(index + ODD_AHEAD, 1)

    own = jnp.where(b < middle, 0, middle)
    own_pair = pl.ds(own, middle)
    other_pair = pl.ds(middle - own, middle)
    near = 2 * own + 1 - b
    inward = jnp.where(b < middle, middle - 1, middle)
    team = middle * cols
    place = (b - own) * cols + c
    across = blocks - 1 - b
    inner = jnp.logical_and(b >= middle - 1, b <= middle)

    def chain(stage, peer, blocks_of):
        remote(
            {"blk": peer},
            spline.at[c, blocks_of],
            spline.at[c, blocks_of],
            chain_send.at[stage],
            chain_recv.at[stage],
        ).start()

    def mode_chain(stage, peer, blocks_of):
        remote(
            {"blk": peer},
            mode_rows.at[dof_span, blocks_of],
            mode_rows.at[dof_span, blocks_of],
            mode_send.at[stage],
            mode_recv.at[stage],
        ).start()

    def await_chain(stage, count):
        settle(spline.at[c, pl.ds(0, count)], chain_recv.at[stage])

        @pl.when(sends_modes)
        def _():
            settle(mode_rows.at[dof_span, pl.ds(0, count)], mode_recv.at[stage])

    def first_stage_modes():
        @pl.when(sends_modes)
        def _():
            remote(
                {"blk": near},
                node_modes.at[dof_span],
                mode_rows.at[dof_span, b],
                mode_send.at[0],
                mode_recv.at[0],
            ).start()

    def second_stage():
        await_chain(0, 1)

        @pl.when(sends_modes)
        def _():
            own_modes.wait()

        @pl.when(inner)
        def _():
            chain(1, across, own_pair)

            @pl.when(sends_modes)
            def _():
                mode_chain(1, across, own_pair)

    def third_stage():
        @pl.when(inner)
        def _():
            await_chain(1, middle)
            chain(2, near, other_pair)

            @pl.when(sends_modes)
            def _():
                mode_chain(2, near, other_pair)

            share_lists()

    def last_stage():
        @pl.when(jnp.logical_not(inner))
        def _():
            await_chain(2, middle)
            share_lists()

    def share_lists():
        for k in range(1, cols):
            remote(
                {"col": on_plane(k)},
                spline.at[c],
                spline.at[c],
                spline_send,
                spline_recv,
            ).start()

        @pl.when(sends_modes)
        def _():
            for k in range(1, cols):
                remote(
                    {"col": on_plane(k)},
                    mode_rows.at[dof_span],
                    mode_rows.at[dof_span],
                    mode_send.at[2 + k],
                    mode_plane_recv.at[c // half],
                ).start()

    first_stage_modes()
    for index in range(OPENING):
        send_piece(index, 0)
        send_piece(index, 1)

    row_at = lax.broadcasted_iota(jnp.int32, (sub, length), 0)
    column_at = lax.broadcasted_iota(jnp.int32, (sub, length), 1)
    total = jnp.zeros((sub, length), jnp.float32)
    for copy in list_copies:
        copy.wait()
    for o in range(owners):
        for s in range(slots):
            live = s < counts[0, 0, o]
            row = jnp.where(live, rows_list[0, 0, o, s], -1)
            node = nodes_list[0, 0, o, s] + o * node_count
            spread = jnp.zeros((sub, length), jnp.float32)
            for d in range(dofs):
                spread = jnp.where(
                    column_at == node + d * owners * node_count,
                    weights[0, 0, d, o, s],
                    spread,
                )
            total = total + jnp.where(row_at == row, spread, 0.0)
    spline[c, b] = total
    remote(
        {"blk": near}, spline.at[c, b], spline.at[c, b], chain_send.at[0], chain_recv.at[0]
    ).start()
    for index in range(OPENING, max(AHEAD, ODD_AHEAD)):
        if index < AHEAD:
            send_piece(index, 0)
        if index < ODD_AHEAD:
            send_piece(index, 1)

    for p in range(stripes):
        panel_copies[p].wait()
        where = pl.ds(p * stripe, stripe)
        high, low = split(shapes[where])
        shapes_high[where] = high
        shapes_low[where] = low

    def multiply(q, start, stop):
        where = pl.ds(start * span, (stop - start) * span)
        lines = blocks * sub
        high, low = split(influence[q, :, :, where].reshape(lines, (stop - start) * span))
        product = jnp.dot(
            jnp.concatenate([high, low], axis=0),
            shapes_high[where],
            preferred_element_type=jnp.float32,
        )
        rest = jnp.dot(high, shapes_low[where], preferred_element_type=jnp.float32)
        return product[:lines] + (product[lines:] + rest)

    def to_half(q):
        partial[q] = multiply(q, 0, parts).reshape(blocks, sub, width)
        for r in range(cols):

            @pl.when(jnp.logical_or(b != inward, c != r))
            def _():
                remote(
                    {"blk": inward, "col": r},
                    partial.at[q, r],
                    half_in.at[q, place],
                    half_send,
                    half_recv.at[q],
                ).start()

        @pl.when(inner)
        def _():
            half_in[q, place] = partial[q, c]

    def half_sum(q):
        @pl.when(inner)
        def _():
            settle(half_in.at[q, pl.ds(0, team - 1)], half_recv.at[q])
            total = half_in[q, 0]
            for source in range(1, team):
                total = total + half_in[q, source]
            half_out[q] = total
            remote(
                {"blk": across}, half_out.at[q], cross_in.at[q], cross_send, cross_recv.at[q]
            ).start()

    def full_sum(q):
        @pl.when(inner)
        def _():
            settle(cross_in.at[q], cross_recv.at[q])
            pressure[q, c] = half_out[q] + cross_in[q]
            for peer in (near, b):
                for k in range(cols):
                    if peer is b and k == 0:
                        continue
                    remote(
                        {"blk": peer, "col": on_plane(k)},
                        pressure.at[q, c],
                        pressure.at[q, c],
                        final_send,
                        final_recv.at[q],
                    ).start()

    def await_final(q):
        @pl.when(inner)
        def _():
            settle(pressure.at[q, pl.ds(0, cols - 1)], final_recv.at[q])

        @pl.when(jnp.logical_not(inner))
        def _():
            settle(pressure.at[q], final_recv.at[q])

    def seat(r):
        return middle - 1 + r % 2

    is_owner = b == middle - 1 + lax.rem(c, 2)

    def to_owners():
        for r in range(cols):

            @pl.when(jnp.logical_or(b != seat(r), c != r))
            def _():
                remote(
                    {"blk": seat(r), "col": r},
                    partial.at[last, r],
                    gather_in.at[b * cols + c],
                    gather_send,
                    gather_recv,
                ).start()

    def cast():
        @pl.when(is_owner)
        def _():
            gather_in[b * cols + c] = partial[last, c]
            settle(gather_in.at[pl.ds(0, blocks * cols - 1)], gather_recv)
            total = gather_in[0]
            for source in range(1, blocks * cols):
                total = total + gather_in[source]
            pressure[last, c] = total
            for j in range(blocks):
                for k in range(cols):
                    if j == blocks - 1 and k == 0:
                        continue
                    peer = b if j == blocks - 1 else far_target(j)
                    remote(
                        {"blk": peer, "col": on_plane(k)},
                        pressure.at[last, c],
                        pressure.at[last, c],
                        cast_send,
                        cast_recv,
                    ).start()

    def await_cast():
        @pl.when(is_owner)
        def _():
            settle(pressure.at[last, pl.ds(0, cols - 1)], cast_recv)

        @pl.when(jnp.logical_not(is_owner))
        def _():
            settle(pressure.at[last], cast_recv)

    def make_force():
        settle(spline.at[pl.ds(0, cols - 1)], spline_recv)
        for s in range(2):

            @pl.when(c != s * half + half - 1)
            def _():
                settle(mode_rows.at[pl.ds(s * share, share)], mode_plane_recv.at[s])

        force[...] = jnp.dot(
            spline[...].reshape(cols * blocks * sub, length),
            mode_rows[...].reshape(length, modes),
            precision=HIGHEST,
            preferred_element_type=jnp.float32,
        )

    def modal(start, stop):
        rows = (stop - start) * blocks * sub
        force_high, force_low = split(force[pl.ds(start * blocks * sub, rows)])
        high, low = split(pressure[start:stop].reshape(rows, width))
        return lax.dot_general(
            jnp.concatenate([force_high, force_high, force_low], axis=0),
            jnp.concatenate([high, low, high], axis=0),
            (((0,), (0,)), ((), ())),
            preferred_element_type=jnp.float32,
        )

    for index in range(total_pieces):
        await_piece(index)
        q, h = divmod(index, parts)
        if q == last:
            product = multiply(last, h, h + 1)
            ending = product if h == 0 else ending + product
        elif h == parts - 1:
            to_half(q)
        if index == SECOND_AT:
            second_stage()
        if index == THIRD_AT:
            third_stage()
        if index == LAST_AT:
            last_stage()
        for kind, q in AFTER.get(index, ()):
            (half_sum, full_sum)[kind](q)
    partial[last] = ending.reshape(blocks, sub, width)
    to_owners()
    if LAST_AT is None:
        last_stage()
    for kind, q in TAIL:
        (half_sum, full_sum)[kind](q)
    cast()
    for kind, q in FINAL:
        (half_sum, full_sum)[kind](q)
    make_force()
    for q in early:
        await_final(q)
    out[...] = modal(0, last)
    await_cast()
    out[...] += modal(last, chunks)

    settle(influence.at[pl.ds(0, blocks - 1)], aic_send)
    settle(spline.at[c, 0], chain_send.at[0])

    @pl.when(inner)
    def _():
        settle(spline.at[c, pl.ds(0, middle)], chain_send.at[1])
        settle(spline.at[c, pl.ds(0, middle)], chain_send.at[2])

    settle(spline.at[pl.ds(0, cols - 1)], spline_send)
    @pl.when(inner)
    def _():
        settle(partial.at[pl.ds(0, last), pl.ds(0, cols - 1)], half_send)
        settle(half_out, cross_send)
        settle(half_in.at[:, pl.ds(0, team - 1)], final_send)

    @pl.when(jnp.logical_not(inner))
    def _():
        settle(partial.at[pl.ds(0, last)], half_send)

    @pl.when(is_owner)
    def _():
        settle(partial.at[last, pl.ds(0, cols - 1)], gather_send)
        settle(gather_in.at[pl.ds(0, blocks * cols - 1)], cast_send)

    @pl.when(jnp.logical_not(is_owner))
    def _():
        settle(partial.at[last], gather_send)

    @pl.when(sends_modes)
    def _():
        settle(mode_rows.at[dof_span, 0], mode_send.at[0])

        @pl.when(inner)
        def _():
            settle(mode_rows.at[dof_span, pl.ds(0, middle)], mode_send.at[1])
            settle(mode_rows.at[dof_span, pl.ds(0, middle)], mode_send.at[2])

        for k in range(1, cols):
            settle(mode_rows.at[dof_span], mode_send.at[2 + k])


def by_kernel(aic, downwash, node_modes, src_rows, dst_nodes, counts, spline_weights):
    blocks = lax.axis_size("blk")
    cols = lax.axis_size("col")
    rows = aic.shape[0]
    sub = rows // cols
    depth, width = downwash.shape[1:]
    dofs, node_count, modes = node_modes.shape
    length = dofs * blocks * node_count
    stripes = 4
    dma = pltpu.SemaphoreType.DMA
    anywhere = pl.BlockSpec(memory_space=pl.ANY)
    operands = (aic, downwash, node_modes, src_rows, dst_nodes, counts, spline_weights)
    in_hbm = [pltpu.with_memory_space_constraint(v, pltpu.MemorySpace.HBM) for v in operands]
    return pl.pallas_call(
        functools.partial(exchange_kernel, blocks, cols),
        name="gaf_exchange",
        out_shape=jax.ShapeDtypeStruct((modes, width), jnp.float32),
        in_specs=[anywhere] * 7,
        out_specs=pl.BlockSpec(memory_space=pltpu.VMEM),
        scratch_shapes=[
            pltpu.VMEM((cols, blocks, sub, depth), jnp.float32),
            pltpu.VMEM((depth, width), jnp.float32),
            pltpu.VMEM((depth, width), jnp.bfloat16),
            pltpu.VMEM((depth, width), jnp.bfloat16),
            pltpu.VMEM((cols, blocks, sub, width), jnp.float32),
            pltpu.VMEM((cols - 1, blocks // 2 * cols, sub, width), jnp.float32),
            pltpu.VMEM((cols - 1, sub, width), jnp.float32),
            pltpu.VMEM((cols - 1, sub, width), jnp.float32),
            pltpu.VMEM((blocks * cols, sub, width), jnp.float32),
            pltpu.VMEM((cols, blocks, sub, width), jnp.float32),
            pltpu.VMEM((cols, blocks, sub, length), jnp.float32),
            pltpu.VMEM((dofs, blocks, node_count, modes), jnp.float32),
            pltpu.VMEM((cols * blocks * sub, modes), jnp.float32),
            pltpu.SMEM(src_rows.shape, jnp.int32),
            pltpu.SMEM(dst_nodes.shape, jnp.int32),
            pltpu.SMEM(counts.shape, jnp.int32),
            pltpu.SMEM(spline_weights.shape, jnp.float32),
            dma((4,)),
            dma((stripes + 1,)),
            dma((cols * PARTS,)),
            dma,
            dma((cols - 1,)),
            dma,
            dma((cols - 1,)),
            dma,
            dma((cols - 1,)),
            dma,
            dma,
            dma,
            dma,
            dma,
            dma((3,)),
            dma((3,)),
            dma,
            dma,
            dma((3,)),
            dma((2 + cols,)),
            dma((2,)),
        ],
        compiler_params=pltpu.CompilerParams(
            collective_id=0, has_side_effects=True, vmem_limit_bytes=32 * 1024 * 1024
        ),
    )(*in_hbm)


def solution(mesh):
    placed = (
        P(("groups", "blk"), "col"),
        P(("groups", "col"), "blk", None),
        P(None, "blk", None),
        P("blk", "col", None, None),
        P("blk", "col", None, None),
        P("blk", "col", None),
        P("blk", "col", None, None, None),
    )

    def shards(*operands):
        aic, downwash, node_modes = operands[:3]
        blocks, cols = lax.axis_size("blk"), lax.axis_size("col")
        small = blocks * aic.shape[0] <= 2 * node_modes.shape[2]
        even = blocks == cols == 4 and cols % 2 == 0 and node_modes.shape[0] % 2 == 0 and aic.shape[0] % (8 * cols) == 0 and downwash.shape[1] % 512 == 0
        if small and even:
            return by_kernel(*operands)
        return by_rotation(*operands)

    return jax.shard_map(
        shards, mesh=mesh, in_specs=placed, out_specs=P("groups", None), check_vma=False
    )
```

```python
import functools

import jax
import jax.numpy as jnp
from jax import lax
from jax.experimental import pallas as pl
from jax.experimental.pallas import tpu as pltpu
from jax.sharding import PartitionSpec as P


HIGHEST = lax.Precision.HIGHEST
PARTS = 2
AHEAD = 3
SECOND_AT = 1
THIRD_AT = 4
OPENING = 2
LAST_AT = 6
LATE_FROM = 2
AFTER = {4: ((0, 0),), 6: ((0, 1),)}
TAIL = ((1, 0), (1, 1), (1, 2))
FINAL = ()
ODD_AHEAD = 2


def shifted(value, axis, steps):
    count = lax.axis_size(axis)
    pairs = [(source, (source + steps) % count) for source in range(count)]
    return lax.ppermute(value, axis, pairs)


def by_rotation(aic, downwash, node_modes, src_rows, dst_nodes, counts, spline_weights):
    cycle_size = lax.axis_size("blk")
    col_count = lax.axis_size("col")
    device = lax.axis_index("blk")
    own_block = downwash[0]
    panel_rows = own_block.shape[0]

    def product(shapes, source):
        columns = lax.dynamic_slice_in_dim(aic, source * panel_rows, panel_rows, 1)
        return jnp.dot(
            columns, shapes, precision=lax.Precision.HIGHEST, preferred_element_type=jnp.float32
        )

    halfway = cycle_size // 2

    def advance(offset, running):
        pressure, forward, behind = running
        forward = shifted(forward, "blk", 1)
        behind = shifted(behind, "blk", -1)
        pressure = pressure + product(forward, (device - offset) % cycle_size)
        pressure = pressure + product(behind, (device + offset) % cycle_size)
        return (pressure, forward, behind)

    pressure = product(own_block, device)
    pressure, forward, behind = lax.fori_loop(1, halfway, advance, (pressure, own_block, own_block))
    forward = shifted(forward, "blk", 1)
    pressure = pressure + product(forward, (device - halfway) % cycle_size)
    slots = src_rows.shape[-1]
    slot_index = jnp.arange(slots, dtype=jnp.int32)
    all_rows, all_nodes, all_counts = (
        lax.all_gather(src_rows, "col", axis=1, tiled=True),
        lax.all_gather(dst_nodes, "col", axis=1, tiled=True),
        lax.all_gather(counts, "col", axis=1, tiled=True),
    )
    weight_all = lax.all_gather(spline_weights, "col", axis=1, tiled=True)
    sub_rows = pressure.shape[0] // col_count
    offsets = jnp.arange(col_count, dtype=jnp.int32)[:, None, None] * sub_rows
    shifted_rows = all_rows[0] + offsets
    row_ids = jnp.transpose(shifted_rows, (1, 0, 2)).reshape(cycle_size, col_count * slots)
    node_ids = jnp.transpose(all_nodes[0], (1, 0, 2)).reshape(cycle_size, col_count * slots)
    live_sub = (slot_index[None, None, :] < all_counts[0][:, :, None]).astype(jnp.float32)
    live = jnp.transpose(live_sub, (1, 0, 2)).reshape(cycle_size, col_count * slots)
    weight_rows = jnp.transpose(weight_all[0], (1, 2, 0, 3)).reshape(
        6, cycle_size, col_count * slots
    )
    node_count = node_modes.shape[1]
    forces = pressure[row_ids.T]
    picks = (node_ids[None, :, :] == jnp.arange(node_count, dtype=jnp.int32)[:, None, None]).astype(
        jnp.float32
    )
    spread = weight_rows[:, None, :, :] * live[None, None, :, :] * picks[None, :, :, :]
    spread = spread.reshape(6 * node_count, cycle_size, row_ids.shape[1])
    arrived_forces, arrived_spread = (
        lax.all_to_all(forces, "blk", split_axis=1, concat_axis=1, tiled=True),
        lax.all_to_all(spread, "blk", split_axis=1, concat_axis=1, tiled=True),
    )
    loads = jnp.einsum(
        "jsc,csk->jk", arrived_spread, arrived_forces, precision=lax.Precision.HIGHEST
    )
    flat_modes = node_modes.reshape(6 * node_count, node_modes.shape[2])
    modal = jnp.einsum("jm,jk->mk", flat_modes, loads, precision=lax.Precision.HIGHEST)
    return lax.psum(modal, ("blk", "col"))


def split(value):
    high = value.astype(jnp.bfloat16)
    low = (value - high.astype(jnp.float32)).astype(jnp.bfloat16)
    return high, low


def exchange_kernel(
    blocks,
    cols,
    aic,
    panels,
    node_modes,
    rows_hbm,
    nodes_hbm,
    counts_hbm,
    weights_hbm,
    out,
    influence,
    shapes,
    shapes_high,
    shapes_low,
    partial,
    half_in,
    half_out,
    cross_in,
    gather_in,
    pressure,
    spline,
    mode_rows,
    force,
    rows_list,
    nodes_list,
    counts,
    weights,
    list_sem,
    panel_sem,
    aic_recv,
    aic_send,
    half_recv,
    half_send,
    cross_recv,
    cross_send,
    final_recv,
    final_send,
    gather_recv,
    gather_send,
    cast_recv,
    cast_send,
    chain_recv,
    chain_send,
    spline_recv,
    spline_send,
    mode_recv,
    mode_send,
    mode_plane_recv,
):
    b = lax.axis_index("blk")
    c = lax.axis_index("col")
    chunks, _, sub, depth = influence.shape
    dofs, _, node_count, modes = mode_rows.shape
    owners, slots = rows_list.shape[2:]
    width = panels.shape[2]
    last = chunks - 1
    early = range(last)
    parts = PARTS
    span = depth // parts
    total_pieces = chunks * parts
    middle = blocks // 2
    length = dofs * owners * node_count

    def on_line(k):
        return lax.rem(b + k, blocks)

    def on_plane(k):
        return lax.rem(c + k, cols)

    def far_target(j):
        falling = blocks - 1 - j
        rising = j
        falling = jnp.where(falling <= b, falling - 1, falling)
        rising = jnp.where(rising >= b, rising + 1, rising)
        return jnp.where(b < middle, falling, rising)

    def remote(where, source, target, send, recv):
        return pltpu.make_async_remote_copy(
            src_ref=source,
            dst_ref=target,
            send_sem=send,
            recv_sem=recv,
            device_id=where,
            device_id_type=pl.DeviceIdType.MESH,
        )

    def settle(ref, sem):
        pltpu.make_async_copy(ref, ref, sem).wait()

    barrier = pltpu.get_barrier_semaphore()
    for z in range(blocks):
        for x in range(cols):
            if (z == 0) != (x == 0):
                pl.semaphore_signal(
                    barrier,
                    inc=1,
                    device_id={"blk": on_line(z), "col": on_plane(x)},
                    device_id_type=pl.DeviceIdType.MESH,
                )

    list_copies = []
    lists = ((rows_hbm, rows_list), (nodes_hbm, nodes_list), (counts_hbm, counts), (weights_hbm, weights))
    for i, (source, target) in enumerate(lists):
        list_copies.append(pltpu.make_async_copy(source, target, list_sem.at[i]))
        list_copies[-1].start()
    stripes = panel_sem.shape[0] - 1
    stripe = depth // stripes
    panel_copies = []
    for p in range(stripes):
        where = pl.ds(p * stripe, stripe)
        panel_copies.append(
            pltpu.make_async_copy(panels.at[0, where], shapes.at[where], panel_sem.at[p])
        )
        panel_copies[-1].start()

    def piece_of(index):
        q, h = divmod(index, parts)
        return q, pl.ds(h * span, span)

    def aic_piece(index, peer):
        q, h = divmod(index, parts)
        start = pl.multiple_of(peer * depth + h * span, 128)
        return aic.at[pl.ds(q * sub, sub), pl.ds(start, span)]

    for index in range(total_pieces):
        q, where = piece_of(index)
        pltpu.make_async_copy(
            aic_piece(index, b), influence.at[q, b, :, where], aic_recv.at[index]
        ).start()
    half = cols // 2
    share = dofs // 2
    dof_span = pl.ds((c // half) * share, share)
    sends_modes = lax.rem(c, half) == half - 1
    own_modes = pltpu.make_async_copy(
        node_modes.at[dof_span], mode_rows.at[dof_span, b], panel_sem.at[stripes]
    )

    @pl.when(sends_modes)
    def _():
        own_modes.start()

    pl.semaphore_wait(barrier, blocks + cols - 2)

    def send_piece(index, parity):
        if index >= total_pieces:
            return
        q, where = piece_of(index)

        @pl.when(lax.rem(c, 2) == parity)
        def _():
            for j in range(blocks - 1):
                peer = far_target(j)
                remote(
                    {"blk": peer},
                    aic_piece(index, peer),
                    influence.at[q, b, :, where],
                    aic_send,
                    aic_recv.at[index],
                ).start()

    def await_piece(index):
        q, where = piece_of(index)
        settle(influence.at[q, :, :, where], aic_recv.at[index])
        send_piece(index + AHEAD, 0)
        send_piece(index + ODD_AHEAD, 1)

    own = jnp.where(b < middle, 0, middle)
    own_pair = pl.ds(own, middle)
    other_pair = pl.ds(middle - own, middle)
    near = 2 * own + 1 - b
    inward = jnp.where(b < middle, middle - 1, middle)
    team = middle * cols
    place = (b - own) * cols + c
    across = blocks - 1 - b
    inner = jnp.logical_and(b >= middle - 1, b <= middle)

    def chain(stage, peer, blocks_of):
        remote(
            {"blk": peer},
            spline.at[c, blocks_of],
            spline.at[c, blocks_of],
            chain_send.at[stage],
            chain_recv.at[stage],
        ).start()

    def mode_chain(stage, peer, blocks_of):
        remote(
            {"blk": peer},
            mode_rows.at[dof_span, blocks_of],
            mode_rows.at[dof_span, blocks_of],
            mode_send.at[stage],
            mode_recv.at[stage],
        ).start()

    def await_chain(stage, count):
        settle(spline.at[c, pl.ds(0, count)], chain_recv.at[stage])

        @pl.when(sends_modes)
        def _():
            settle(mode_rows.at[dof_span, pl.ds(0, count)], mode_recv.at[stage])

    def first_stage_modes():
        @pl.when(sends_modes)
        def _():
            remote(
                {"blk": near},
                node_modes.at[dof_span],
                mode_rows.at[dof_span, b],
                mode_send.at[0],
                mode_recv.at[0],
            ).start()

    def second_stage():
        await_chain(0, 1)

        @pl.when(sends_modes)
        def _():
            own_modes.wait()

        @pl.when(inner)
        def _():
            chain(1, across, own_pair)

            @pl.when(sends_modes)
            def _():
                mode_chain(1, across, own_pair)

    def third_stage():
        @pl.when(inner)
        def _():
            await_chain(1, middle)
            chain(2, near, other_pair)

            @pl.when(sends_modes)
            def _():
                mode_chain(2, near, other_pair)

            share_lists()

    def last_stage():
        @pl.when(jnp.logical_not(inner))
        def _():
            await_chain(2, middle)
            share_lists()

    def share_lists():
        for k in range(1, cols):
            remote(
                {"col": on_plane(k)},
                spline.at[c],
                spline.at[c],
                spline_send,
                spline_recv,
            ).start()

        @pl.when(sends_modes)
        def _():
            for k in range(1, cols):
                remote(
                    {"col": on_plane(k)},
                    mode_rows.at[dof_span],
                    mode_rows.at[dof_span],
                    mode_send.at[2 + k],
                    mode_plane_recv.at[c // half],
                ).start()

    first_stage_modes()
    for index in range(OPENING):
        send_piece(index, 0)
        send_piece(index, 1)

    row_at = lax.broadcasted_iota(jnp.int32, (sub, length), 0)
    column_at = lax.broadcasted_iota(jnp.int32, (sub, length), 1)
    total = jnp.zeros((sub, length), jnp.float32)
    for copy in list_copies:
        copy.wait()
    for o in range(owners):
        for s in range(slots):
            live = s < counts[0, 0, o]
            row = jnp.where(live, rows_list[0, 0, o, s], -1)
            node = nodes_list[0, 0, o, s] + o * node_count
            spread = jnp.zeros((sub, length), jnp.float32)
            for d in range(dofs):
                spread = jnp.where(
                    column_at == node + d * owners * node_count,
                    weights[0, 0, d, o, s],
                    spread,
                )
            total = total + jnp.where(row_at == row, spread, 0.0)
    spline[c, b] = total
    remote(
        {"blk": near}, spline.at[c, b], spline.at[c, b], chain_send.at[0], chain_recv.at[0]
    ).start()
    for index in range(OPENING, max(AHEAD, ODD_AHEAD)):
        if index < AHEAD:
            send_piece(index, 0)
        if index < ODD_AHEAD:
            send_piece(index, 1)

    for p in range(stripes):
        panel_copies[p].wait()
        where = pl.ds(p * stripe, stripe)
        high, low = split(shapes[where])
        shapes_high[where] = high
        shapes_low[where] = low

    def multiply(q, start, stop):
        where = pl.ds(start * span, (stop - start) * span)
        lines = blocks * sub
        high, low = split(influence[q, :, :, where].reshape(lines, (stop - start) * span))
        product = jnp.dot(
            jnp.concatenate([high, low], axis=0),
            shapes_high[where],
            preferred_element_type=jnp.float32,
        )
        rest = jnp.dot(high, shapes_low[where], preferred_element_type=jnp.float32)
        return product[:lines] + (product[lines:] + rest)

    def to_half(q):
        partial[q] = multiply(q, 0, parts).reshape(blocks, sub, width)
        for r in range(cols):

            @pl.when(jnp.logical_or(b != inward, c != r))
            def _():
                remote(
                    {"blk": inward, "col": r},
                    partial.at[q, r],
                    half_in.at[q, place],
                    half_send,
                    half_recv.at[q],
                ).start()

        @pl.when(inner)
        def _():
            half_in[q, place] = partial[q, c]

    def half_sum(q):
        @pl.when(inner)
        def _():
            settle(half_in.at[q, pl.ds(0, team - 1)], half_recv.at[q])
            total = half_in[q, 0]
            for source in range(1, team):
                total = total + half_in[q, source]
            half_out[q] = total
            remote(
                {"blk": across}, half_out.at[q], cross_in.at[q], cross_send, cross_recv.at[q]
            ).start()

    def full_sum(q):
        @pl.when(inner)
        def _():
            settle(cross_in.at[q], cross_recv.at[q])
            pressure[q, c] = half_out[q] + cross_in[q]
            for peer in (near, b):
                for k in range(cols):
                    if peer is b and k == 0:
                        continue
                    remote(
                        {"blk": peer, "col": on_plane(k)},
                        pressure.at[q, c],
                        pressure.at[q, c],
                        final_send,
                        final_recv.at[q],
                    ).start()

    def await_final(q):
        @pl.when(inner)
        def _():
            settle(pressure.at[q, pl.ds(0, cols - 1)], final_recv.at[q])

        @pl.when(jnp.logical_not(inner))
        def _():
            settle(pressure.at[q], final_recv.at[q])

    def seat(r):
        return middle - 1 + r % 2

    is_owner = b == middle - 1 + lax.rem(c, 2)

    def to_owners():
        for r in range(cols):

            @pl.when(jnp.logical_or(b != seat(r), c != r))
            def _():
                remote(
                    {"blk": seat(r), "col": r},
                    partial.at[last, r],
                    gather_in.at[b * cols + c],
                    gather_send,
                    gather_recv,
                ).start()

    def cast():
        @pl.when(is_owner)
        def _():
            gather_in[b * cols + c] = partial[last, c]
            settle(gather_in.at[pl.ds(0, blocks * cols - 1)], gather_recv)
            total = gather_in[0]
            for source in range(1, blocks * cols):
                total = total + gather_in[source]
            pressure[last, c] = total
            for j in range(blocks):
                for k in range(cols):
                    if j == blocks - 1 and k == 0:
                        continue
                    peer = b if j == blocks - 1 else far_target(j)
                    remote(
                        {"blk": peer, "col": on_plane(k)},
                        pressure.at[last, c],
                        pressure.at[last, c],
                        cast_send,
                        cast_recv,
                    ).start()

    def await_cast():
        @pl.when(is_owner)
        def _():
            settle(pressure.at[last, pl.ds(0, cols - 1)], cast_recv)

        @pl.when(jnp.logical_not(is_owner))
        def _():
            settle(pressure.at[last], cast_recv)

    def make_force():
        settle(spline.at[pl.ds(0, cols - 1)], spline_recv)
        for s in range(2):

            @pl.when(c != s * half + half - 1)
            def _():
                settle(mode_rows.at[pl.ds(s * share, share)], mode_plane_recv.at[s])

        force[...] = jnp.dot(
            spline[...].reshape(cols * blocks * sub, length),
            mode_rows[...].reshape(length, modes),
            precision=HIGHEST,
            preferred_element_type=jnp.float32,
        )

    def modal(start, stop):
        rows = (stop - start) * blocks * sub
        force_high, force_low = split(force[pl.ds(start * blocks * sub, rows)])
        high, low = split(pressure[start:stop].reshape(rows, width))
        return lax.dot_general(
            jnp.concatenate([force_high, force_high, force_low], axis=0),
            jnp.concatenate([high, low, high], axis=0),
            (((0,), (0,)), ((), ())),
            preferred_element_type=jnp.float32,
        )

    for index in range(total_pieces):
        await_piece(index)
        q, h = divmod(index, parts)
        if q == last:
            product = multiply(last, h, h + 1)
            ending = product if h == 0 else ending + product
        elif h == parts - 1:
            to_half(q)
        if index == SECOND_AT:
            second_stage()
        if index == THIRD_AT:
            third_stage()
        if index == LAST_AT:
            last_stage()
        for kind, q in AFTER.get(index, ()):
            (half_sum, full_sum)[kind](q)
    partial[last] = ending.reshape(blocks, sub, width)
    if LAST_AT is None:
        last_stage()
    half_sum(last - 1)
    to_owners()
    for kind, q in TAIL:
        (half_sum, full_sum)[kind](q)
    cast()
    for kind, q in FINAL:
        (half_sum, full_sum)[kind](q)
    make_force()
    for q in range(LATE_FROM):
        await_final(q)
    out[...] = modal(0, LATE_FROM)
    for q in range(LATE_FROM, last):
        await_final(q)
    await_cast()
    out[...] += modal(LATE_FROM, chunks)

    settle(influence.at[pl.ds(0, blocks - 1)], aic_send)
    settle(spline.at[c, 0], chain_send.at[0])

    @pl.when(inner)
    def _():
        settle(spline.at[c, pl.ds(0, middle)], chain_send.at[1])
        settle(spline.at[c, pl.ds(0, middle)], chain_send.at[2])

    settle(spline.at[pl.ds(0, cols - 1)], spline_send)
    @pl.when(inner)
    def _():
        settle(partial.at[pl.ds(0, last), pl.ds(0, cols - 1)], half_send)
        settle(half_out, cross_send)
        settle(half_in.at[:, pl.ds(0, team - 1)], final_send)

    @pl.when(jnp.logical_not(inner))
    def _():
        settle(partial.at[pl.ds(0, last)], half_send)

    @pl.when(is_owner)
    def _():
        settle(partial.at[last, pl.ds(0, cols - 1)], gather_send)
        settle(gather_in.at[pl.ds(0, blocks * cols - 1)], cast_send)

    @pl.when(jnp.logical_not(is_owner))
    def _():
        settle(partial.at[last], gather_send)

    @pl.when(sends_modes)
    def _():
        settle(mode_rows.at[dof_span, 0], mode_send.at[0])

        @pl.when(inner)
        def _():
            settle(mode_rows.at[dof_span, pl.ds(0, middle)], mode_send.at[1])
            settle(mode_rows.at[dof_span, pl.ds(0, middle)], mode_send.at[2])

        for k in range(1, cols):
            settle(mode_rows.at[dof_span], mode_send.at[2 + k])


def by_kernel(aic, downwash, node_modes, src_rows, dst_nodes, counts, spline_weights):
    blocks = lax.axis_size("blk")
    cols = lax.axis_size("col")
    rows = aic.shape[0]
    sub = rows // cols
    depth, width = downwash.shape[1:]
    dofs, node_count, modes = node_modes.shape
    length = dofs * blocks * node_count
    stripes = 4
    dma = pltpu.SemaphoreType.DMA
    anywhere = pl.BlockSpec(memory_space=pl.ANY)
    operands = (aic, downwash, node_modes, src_rows, dst_nodes, counts, spline_weights)
    in_hbm = [pltpu.with_memory_space_constraint(v, pltpu.MemorySpace.HBM) for v in operands]
    return pl.pallas_call(
        functools.partial(exchange_kernel, blocks, cols),
        name="gaf_exchange",
        out_shape=jax.ShapeDtypeStruct((modes, width), jnp.float32),
        in_specs=[anywhere] * 7,
        out_specs=pl.BlockSpec(memory_space=pltpu.VMEM),
        scratch_shapes=[
            pltpu.VMEM((cols, blocks, sub, depth), jnp.float32),
            pltpu.VMEM((depth, width), jnp.float32),
            pltpu.VMEM((depth, width), jnp.bfloat16),
            pltpu.VMEM((depth, width), jnp.bfloat16),
            pltpu.VMEM((cols, blocks, sub, width), jnp.float32),
            pltpu.VMEM((cols - 1, blocks // 2 * cols, sub, width), jnp.float32),
            pltpu.VMEM((cols - 1, sub, width), jnp.float32),
            pltpu.VMEM((cols - 1, sub, width), jnp.float32),
            pltpu.VMEM((blocks * cols, sub, width), jnp.float32),
            pltpu.VMEM((cols, blocks, sub, width), jnp.float32),
            pltpu.VMEM((cols, blocks, sub, length), jnp.float32),
            pltpu.VMEM((dofs, blocks, node_count, modes), jnp.float32),
            pltpu.VMEM((cols * blocks * sub, modes), jnp.float32),
            pltpu.SMEM(src_rows.shape, jnp.int32),
            pltpu.SMEM(dst_nodes.shape, jnp.int32),
            pltpu.SMEM(counts.shape, jnp.int32),
            pltpu.SMEM(spline_weights.shape, jnp.float32),
            dma((4,)),
            dma((stripes + 1,)),
            dma((cols * PARTS,)),
            dma,
            dma((cols - 1,)),
            dma,
            dma((cols - 1,)),
            dma,
            dma((cols - 1,)),
            dma,
            dma,
            dma,
            dma,
            dma,
            dma((3,)),
            dma((3,)),
            dma,
            dma,
            dma((3,)),
            dma((2 + cols,)),
            dma((2,)),
        ],
        compiler_params=pltpu.CompilerParams(
            collective_id=0, has_side_effects=True, vmem_limit_bytes=32 * 1024 * 1024
        ),
    )(*in_hbm)


def solution(mesh):
    placed = (
        P(("groups", "blk"), "col"),
        P(("groups", "col"), "blk", None),
        P(None, "blk", None),
        P("blk", "col", None, None),
        P("blk", "col", None, None),
        P("blk", "col", None),
        P("blk", "col", None, None, None),
    )

    def shards(*operands):
        aic, downwash, node_modes = operands[:3]
        blocks, cols = lax.axis_size("blk"), lax.axis_size("col")
        small = blocks * aic.shape[0] <= 2 * node_modes.shape[2]
        even = blocks == cols == 4 and cols % 2 == 0 and node_modes.shape[0] % 2 == 0 and aic.shape[0] % (8 * cols) == 0 and downwash.shape[1] % 512 == 0
        if small and even:
            return by_kernel(*operands)
        return by_rotation(*operands)

    return jax.shard_map(
        shards, mesh=mesh, in_specs=placed, out_specs=P("groups", None), check_vma=False
    )
```

```python
import functools

import jax
import jax.numpy as jnp
from jax import lax
from jax.experimental import pallas as pl
from jax.experimental.pallas import tpu as pltpu
from jax.sharding import PartitionSpec as P


HIGHEST = lax.Precision.HIGHEST
PARTS = 2
AHEAD = 3
SECOND_AT = 1
THIRD_AT = 4
OPENING = 2
LAST_AT = 6
LATE_FROM = 2
AFTER = {4: ((0, 0),), 6: ((0, 1),)}
TAIL = ((0, 2), (1, 0), (1, 1), (1, 2))
FINAL = ()
ODD_AHEAD = 2


def shifted(value, axis, steps):
    count = lax.axis_size(axis)
    pairs = [(source, (source + steps) % count) for source in range(count)]
    return lax.ppermute(value, axis, pairs)


def by_rotation(aic, downwash, node_modes, src_rows, dst_nodes, counts, spline_weights):
    cycle_size = lax.axis_size("blk")
    col_count = lax.axis_size("col")
    device = lax.axis_index("blk")
    own_block = downwash[0]
    panel_rows = own_block.shape[0]

    def product(shapes, source):
        columns = lax.dynamic_slice_in_dim(aic, source * panel_rows, panel_rows, 1)
        return jnp.dot(
            columns, shapes, precision=lax.Precision.HIGHEST, preferred_element_type=jnp.float32
        )

    halfway = cycle_size // 2

    def advance(offset, running):
        pressure, forward, behind = running
        forward = shifted(forward, "blk", 1)
        behind = shifted(behind, "blk", -1)
        pressure = pressure + product(forward, (device - offset) % cycle_size)
        pressure = pressure + product(behind, (device + offset) % cycle_size)
        return (pressure, forward, behind)

    pressure = product(own_block, device)
    pressure, forward, behind = lax.fori_loop(1, halfway, advance, (pressure, own_block, own_block))
    forward = shifted(forward, "blk", 1)
    pressure = pressure + product(forward, (device - halfway) % cycle_size)
    slots = src_rows.shape[-1]
    slot_index = jnp.arange(slots, dtype=jnp.int32)
    all_rows, all_nodes, all_counts = (
        lax.all_gather(src_rows, "col", axis=1, tiled=True),
        lax.all_gather(dst_nodes, "col", axis=1, tiled=True),
        lax.all_gather(counts, "col", axis=1, tiled=True),
    )
    weight_all = lax.all_gather(spline_weights, "col", axis=1, tiled=True)
    sub_rows = pressure.shape[0] // col_count
    offsets = jnp.arange(col_count, dtype=jnp.int32)[:, None, None] * sub_rows
    shifted_rows = all_rows[0] + offsets
    row_ids = jnp.transpose(shifted_rows, (1, 0, 2)).reshape(cycle_size, col_count * slots)
    node_ids = jnp.transpose(all_nodes[0], (1, 0, 2)).reshape(cycle_size, col_count * slots)
    live_sub = (slot_index[None, None, :] < all_counts[0][:, :, None]).astype(jnp.float32)
    live = jnp.transpose(live_sub, (1, 0, 2)).reshape(cycle_size, col_count * slots)
    weight_rows = jnp.transpose(weight_all[0], (1, 2, 0, 3)).reshape(
        6, cycle_size, col_count * slots
    )
    node_count = node_modes.shape[1]
    forces = pressure[row_ids.T]
    picks = (node_ids[None, :, :] == jnp.arange(node_count, dtype=jnp.int32)[:, None, None]).astype(
        jnp.float32
    )
    spread = weight_rows[:, None, :, :] * live[None, None, :, :] * picks[None, :, :, :]
    spread = spread.reshape(6 * node_count, cycle_size, row_ids.shape[1])
    arrived_forces, arrived_spread = (
        lax.all_to_all(forces, "blk", split_axis=1, concat_axis=1, tiled=True),
        lax.all_to_all(spread, "blk", split_axis=1, concat_axis=1, tiled=True),
    )
    loads = jnp.einsum(
        "jsc,csk->jk", arrived_spread, arrived_forces, precision=lax.Precision.HIGHEST
    )
    flat_modes = node_modes.reshape(6 * node_count, node_modes.shape[2])
    modal = jnp.einsum("jm,jk->mk", flat_modes, loads, precision=lax.Precision.HIGHEST)
    return lax.psum(modal, ("blk", "col"))


def split(value):
    high = value.astype(jnp.bfloat16)
    low = (value - high.astype(jnp.float32)).astype(jnp.bfloat16)
    return high, low


def exchange_kernel(
    blocks,
    cols,
    aic,
    panels,
    node_modes,
    rows_hbm,
    nodes_hbm,
    counts_hbm,
    weights_hbm,
    out,
    influence,
    shapes,
    shapes_high,
    shapes_low,
    partial,
    half_in,
    half_out,
    cross_in,
    gather_in,
    pressure,
    spline,
    mode_rows,
    force,
    rows_list,
    nodes_list,
    counts,
    weights,
    list_sem,
    panel_sem,
    aic_recv,
    aic_send,
    half_recv,
    half_send,
    cross_recv,
    cross_send,
    final_recv,
    final_send,
    gather_recv,
    gather_send,
    cast_recv,
    cast_send,
    chain_recv,
    chain_send,
    spline_recv,
    spline_send,
    mode_recv,
    mode_send,
    mode_plane_recv,
):
    b = lax.axis_index("blk")
    c = lax.axis_index("col")
    chunks, _, sub, depth = influence.shape
    dofs, _, node_count, modes = mode_rows.shape
    owners, slots = rows_list.shape[2:]
    width = panels.shape[2]
    last = chunks - 1
    early = range(last)
    parts = PARTS
    span = depth // parts
    total_pieces = chunks * parts
    middle = blocks // 2
    length = dofs * owners * node_count

    def on_line(k):
        return lax.rem(b + k, blocks)

    def on_plane(k):
        return lax.rem(c + k, cols)

    def far_target(j):
        falling = blocks - 1 - j
        rising = j
        falling = jnp.where(falling <= b, falling - 1, falling)
        rising = jnp.where(rising >= b, rising + 1, rising)
        return jnp.where(b < middle, falling, rising)

    def remote(where, source, target, send, recv):
        return pltpu.make_async_remote_copy(
            src_ref=source,
            dst_ref=target,
            send_sem=send,
            recv_sem=recv,
            device_id=where,
            device_id_type=pl.DeviceIdType.MESH,
        )

    def settle(ref, sem):
        pltpu.make_async_copy(ref, ref, sem).wait()

    barrier = pltpu.get_barrier_semaphore()
    for z in range(blocks):
        for x in range(cols):
            if (z == 0) != (x == 0):
                pl.semaphore_signal(
                    barrier,
                    inc=1,
                    device_id={"blk": on_line(z), "col": on_plane(x)},
                    device_id_type=pl.DeviceIdType.MESH,
                )

    list_copies = []
    lists = ((rows_hbm, rows_list), (nodes_hbm, nodes_list), (counts_hbm, counts), (weights_hbm, weights))
    for i, (source, target) in enumerate(lists):
        list_copies.append(pltpu.make_async_copy(source, target, list_sem.at[i]))
        list_copies[-1].start()
    stripes = panel_sem.shape[0] - 1
    stripe = depth // stripes
    panel_copies = []
    for p in range(stripes):
        where = pl.ds(p * stripe, stripe)
        panel_copies.append(
            pltpu.make_async_copy(panels.at[0, where], shapes.at[where], panel_sem.at[p])
        )
        panel_copies[-1].start()

    def piece_of(index):
        q, h = divmod(index, parts)
        return q, pl.ds(h * span, span)

    def aic_piece(index, peer):
        q, h = divmod(index, parts)
        start = pl.multiple_of(peer * depth + h * span, 128)
        return aic.at[pl.ds(q * sub, sub), pl.ds(start, span)]

    for index in range(total_pieces):
        q, where = piece_of(index)
        pltpu.make_async_copy(
            aic_piece(index, b), influence.at[q, b, :, where], aic_recv.at[index]
        ).start()
    half = cols // 2
    share = dofs // 2
    dof_span = pl.ds((c // half) * share, share)
    sends_modes = lax.rem(c, half) == half - 1
    own_modes = pltpu.make_async_copy(
        node_modes.at[dof_span], mode_rows.at[dof_span, b], panel_sem.at[stripes]
    )

    @pl.when(sends_modes)
    def _():
        own_modes.start()

    pl.semaphore_wait(barrier, blocks + cols - 2)

    def send_piece(index, parity):
        if index >= total_pieces:
            return
        q, where = piece_of(index)

        @pl.when(lax.rem(c, 2) == parity)
        def _():
            for j in range(blocks - 1):
                peer = far_target(j)
                remote(
                    {"blk": peer},
                    aic_piece(index, peer),
                    influence.at[q, b, :, where],
                    aic_send,
                    aic_recv.at[index],
                ).start()

    def await_piece(index):
        q, where = piece_of(index)
        settle(influence.at[q, :, :, where], aic_recv.at[index])
        send_piece(index + AHEAD, 0)
        send_piece(index + ODD_AHEAD, 1)

    own = jnp.where(b < middle, 0, middle)
    own_pair = pl.ds(own, middle)
    other_pair = pl.ds(middle - own, middle)
    near = 2 * own + 1 - b
    inward = jnp.where(b < middle, middle - 1, middle)
    team = middle * cols
    place = (b - own) * cols + c
    across = blocks - 1 - b
    inner = jnp.logical_and(b >= middle - 1, b <= middle)

    def chain(stage, peer, blocks_of):
        remote(
            {"blk": peer},
            spline.at[c, blocks_of],
            spline.at[c, blocks_of],
            chain_send.at[stage],
            chain_recv.at[stage],
        ).start()

    def mode_chain(stage, peer, blocks_of):
        remote(
            {"blk": peer},
            mode_rows.at[dof_span, blocks_of],
            mode_rows.at[dof_span, blocks_of],
            mode_send.at[stage],
            mode_recv.at[stage],
        ).start()

    def await_chain(stage, count):
        settle(spline.at[c, pl.ds(0, count)], chain_recv.at[stage])

        @pl.when(sends_modes)
        def _():
            settle(mode_rows.at[dof_span, pl.ds(0, count)], mode_recv.at[stage])

    def first_stage_modes():
        @pl.when(sends_modes)
        def _():
            remote(
                {"blk": near},
                node_modes.at[dof_span],
                mode_rows.at[dof_span, b],
                mode_send.at[0],
                mode_recv.at[0],
            ).start()

    def second_stage():
        await_chain(0, 1)

        @pl.when(sends_modes)
        def _():
            own_modes.wait()

        @pl.when(inner)
        def _():
            chain(1, across, own_pair)

            @pl.when(sends_modes)
            def _():
                mode_chain(1, across, own_pair)

    def third_stage():
        @pl.when(inner)
        def _():
            await_chain(1, middle)
            chain(2, near, other_pair)

            @pl.when(sends_modes)
            def _():
                mode_chain(2, near, other_pair)

            share_lists()

    def last_stage():
        @pl.when(jnp.logical_not(inner))
        def _():
            await_chain(2, middle)
            share_lists()

    def share_lists():
        for k in range(1, cols):
            remote(
                {"col": on_plane(k)},
                spline.at[c],
                spline.at[c],
                spline_send,
                spline_recv,
            ).start()

        @pl.when(sends_modes)
        def _():
            for k in range(1, cols):
                remote(
                    {"col": on_plane(k)},
                    mode_rows.at[dof_span],
                    mode_rows.at[dof_span],
                    mode_send.at[2 + k],
                    mode_plane_recv.at[c // half],
                ).start()

    first_stage_modes()
    for index in range(OPENING):
        send_piece(index, 0)
        send_piece(index, 1)

    row_at = lax.broadcasted_iota(jnp.int32, (sub, length), 0)
    column_at = lax.broadcasted_iota(jnp.int32, (sub, length), 1)
    total = jnp.zeros((sub, length), jnp.float32)
    for copy in list_copies:
        copy.wait()
    for o in range(owners):
        for s in range(slots):
            live = s < counts[0, 0, o]
            row = jnp.where(live, rows_list[0, 0, o, s], -1)
            node = nodes_list[0, 0, o, s] + o * node_count
            spread = jnp.zeros((sub, length), jnp.float32)
            for d in range(dofs):
                spread = jnp.where(
                    column_at == node + d * owners * node_count,
                    weights[0, 0, d, o, s],
                    spread,
                )
            total = total + jnp.where(row_at == row, spread, 0.0)
    spline[c, b] = total
    remote(
        {"blk": near}, spline.at[c, b], spline.at[c, b], chain_send.at[0], chain_recv.at[0]
    ).start()
    for index in range(OPENING, max(AHEAD, ODD_AHEAD)):
        if index < AHEAD:
            send_piece(index, 0)
        if index < ODD_AHEAD:
            send_piece(index, 1)

    for p in range(stripes):
        panel_copies[p].wait()
        where = pl.ds(p * stripe, stripe)
        high, low = split(shapes[where])
        shapes_high[where] = high
        shapes_low[where] = low

    def multiply(q, start, stop):
        where = pl.ds(start * span, (stop - start) * span)
        lines = blocks * sub
        high, low = split(influence[q, :, :, where].reshape(lines, (stop - start) * span))
        product = jnp.dot(
            jnp.concatenate([high, low], axis=0),
            shapes_high[where],
            preferred_element_type=jnp.float32,
        )
        rest = jnp.dot(high, shapes_low[where], preferred_element_type=jnp.float32)
        return product[:lines] + (product[lines:] + rest)

    def to_half(q):
        partial[q] = multiply(q, 0, parts).reshape(blocks, sub, width)
        for r in range(cols):

            @pl.when(jnp.logical_or(b != inward, c != r))
            def _():
                remote(
                    {"blk": inward, "col": r},
                    partial.at[q, r],
                    half_in.at[q, place],
                    half_send,
                    half_recv.at[q],
                ).start()

        @pl.when(inner)
        def _():
            half_in[q, place] = partial[q, c]

    def half_sum(q):
        @pl.when(inner)
        def _():
            settle(half_in.at[q, pl.ds(0, team - 1)], half_recv.at[q])
            total = half_in[q, 0]
            for source in range(1, team):
                total = total + half_in[q, source]
            half_out[q] = total
            remote(
                {"blk": across}, half_out.at[q], cross_in.at[q], cross_send, cross_recv.at[q]
            ).start()

    def full_sum(q):
        @pl.when(inner)
        def _():
            settle(cross_in.at[q], cross_recv.at[q])
            pressure[q, c] = half_out[q] + cross_in[q]
            for peer in (near, b):
                for k in range(cols):
                    if peer is b and k == 0:
                        continue
                    remote(
                        {"blk": peer, "col": on_plane(k)},
                        pressure.at[q, c],
                        pressure.at[q, c],
                        final_send,
                        final_recv.at[q],
                    ).start()

    def await_final(q):
        @pl.when(inner)
        def _():
            settle(pressure.at[q, pl.ds(0, cols - 1)], final_recv.at[q])

        @pl.when(jnp.logical_not(inner))
        def _():
            settle(pressure.at[q], final_recv.at[q])

    def seat(r):
        return middle - 1 + r % 2

    def chair(r):
        return r // 2 * 2 + 1

    is_owner = jnp.logical_and(inner, lax.rem(c, 2) == 1)
    mine = jnp.where(inner, c // 2 * 2 + b - (middle - 1), 0)

    def to_owners():
        for r in range(cols):

            @pl.when(jnp.logical_or(b != seat(r), c != chair(r)))
            def _():
                remote(
                    {"blk": seat(r), "col": chair(r)},
                    partial.at[last, r],
                    gather_in.at[b * cols + c],
                    gather_send,
                    gather_recv,
                ).start()

    def cast():
        @pl.when(is_owner)
        def _():
            gather_in[b * cols + c] = partial[last, mine]
            settle(gather_in.at[pl.ds(0, blocks * cols - 1)], gather_recv)
            total = gather_in[0]
            for source in range(1, blocks * cols):
                total = total + gather_in[source]
            pressure[last, mine] = total
            for j in range(blocks):
                for k in range(cols):
                    if j == blocks - 1 and k == 0:
                        continue
                    peer = b if j == blocks - 1 else far_target(j)
                    remote(
                        {"blk": peer, "col": on_plane(k)},
                        pressure.at[last, mine],
                        pressure.at[last, mine],
                        cast_send,
                        cast_recv,
                    ).start()

    def await_cast():
        @pl.when(is_owner)
        def _():
            settle(pressure.at[last, pl.ds(0, cols - 1)], cast_recv)

        @pl.when(jnp.logical_not(is_owner))
        def _():
            settle(pressure.at[last], cast_recv)

    def make_force():
        settle(spline.at[pl.ds(0, cols - 1)], spline_recv)
        for s in range(2):

            @pl.when(c != s * half + half - 1)
            def _():
                settle(mode_rows.at[pl.ds(s * share, share)], mode_plane_recv.at[s])

        force[...] = jnp.dot(
            spline[...].reshape(cols * blocks * sub, length),
            mode_rows[...].reshape(length, modes),
            precision=HIGHEST,
            preferred_element_type=jnp.float32,
        )

    def modal(start, stop):
        rows = (stop - start) * blocks * sub
        force_high, force_low = split(force[pl.ds(start * blocks * sub, rows)])
        high, low = split(pressure[start:stop].reshape(rows, width))
        return lax.dot_general(
            jnp.concatenate([force_high, force_high, force_low], axis=0),
            jnp.concatenate([high, low, high], axis=0),
            (((0,), (0,)), ((), ())),
            preferred_element_type=jnp.float32,
        )

    for index in range(total_pieces):
        await_piece(index)
        q, h = divmod(index, parts)
        if q == last:
            product = multiply(last, h, h + 1)
            ending = product if h == 0 else ending + product
        elif h == parts - 1:
            to_half(q)
        if index == SECOND_AT:
            second_stage()
        if index == THIRD_AT:
            third_stage()
        if index == LAST_AT:
            last_stage()
        for kind, q in AFTER.get(index, ()):
            (half_sum, full_sum)[kind](q)
    partial[last] = ending.reshape(blocks, sub, width)
    to_owners()
    if LAST_AT is None:
        last_stage()
    for kind, q in TAIL:
        (half_sum, full_sum)[kind](q)
    cast()
    for kind, q in FINAL:
        (half_sum, full_sum)[kind](q)
    make_force()
    for q in range(LATE_FROM):
        await_final(q)
    out[...] = modal(0, LATE_FROM)
    for q in range(LATE_FROM, last):
        await_final(q)
    await_cast()
    out[...] += modal(LATE_FROM, chunks)

    settle(influence.at[pl.ds(0, blocks - 1)], aic_send)
    settle(spline.at[c, 0], chain_send.at[0])

    @pl.when(inner)
    def _():
        settle(spline.at[c, pl.ds(0, middle)], chain_send.at[1])
        settle(spline.at[c, pl.ds(0, middle)], chain_send.at[2])

    settle(spline.at[pl.ds(0, cols - 1)], spline_send)
    @pl.when(inner)
    def _():
        settle(partial.at[pl.ds(0, last), pl.ds(0, cols - 1)], half_send)
        settle(half_out, cross_send)
        settle(half_in.at[:, pl.ds(0, team - 1)], final_send)

    @pl.when(jnp.logical_not(inner))
    def _():
        settle(partial.at[pl.ds(0, last)], half_send)

    @pl.when(is_owner)
    def _():
        settle(partial.at[last, pl.ds(0, cols - 1)], gather_send)
        settle(gather_in.at[pl.ds(0, blocks * cols - 1)], cast_send)

    @pl.when(jnp.logical_not(is_owner))
    def _():
        settle(partial.at[last], gather_send)

    @pl.when(sends_modes)
    def _():
        settle(mode_rows.at[dof_span, 0], mode_send.at[0])

        @pl.when(inner)
        def _():
            settle(mode_rows.at[dof_span, pl.ds(0, middle)], mode_send.at[1])
            settle(mode_rows.at[dof_span, pl.ds(0, middle)], mode_send.at[2])

        for k in range(1, cols):
            settle(mode_rows.at[dof_span], mode_send.at[2 + k])


def by_kernel(aic, downwash, node_modes, src_rows, dst_nodes, counts, spline_weights):
    blocks = lax.axis_size("blk")
    cols = lax.axis_size("col")
    rows = aic.shape[0]
    sub = rows // cols
    depth, width = downwash.shape[1:]
    dofs, node_count, modes = node_modes.shape
    length = dofs * blocks * node_count
    stripes = 4
    dma = pltpu.SemaphoreType.DMA
    anywhere = pl.BlockSpec(memory_space=pl.ANY)
    operands = (aic, downwash, node_modes, src_rows, dst_nodes, counts, spline_weights)
    in_hbm = [pltpu.with_memory_space_constraint(v, pltpu.MemorySpace.HBM) for v in operands]
    return pl.pallas_call(
        functools.partial(exchange_kernel, blocks, cols),
        name="gaf_exchange",
        out_shape=jax.ShapeDtypeStruct((modes, width), jnp.float32),
        in_specs=[anywhere] * 7,
        out_specs=pl.BlockSpec(memory_space=pltpu.VMEM),
        scratch_shapes=[
            pltpu.VMEM((cols, blocks, sub, depth), jnp.float32),
            pltpu.VMEM((depth, width), jnp.float32),
            pltpu.VMEM((depth, width), jnp.bfloat16),
            pltpu.VMEM((depth, width), jnp.bfloat16),
            pltpu.VMEM((cols, blocks, sub, width), jnp.float32),
            pltpu.VMEM((cols - 1, blocks // 2 * cols, sub, width), jnp.float32),
            pltpu.VMEM((cols - 1, sub, width), jnp.float32),
            pltpu.VMEM((cols - 1, sub, width), jnp.float32),
            pltpu.VMEM((blocks * cols, sub, width), jnp.float32),
            pltpu.VMEM((cols, blocks, sub, width), jnp.float32),
            pltpu.VMEM((cols, blocks, sub, length), jnp.float32),
            pltpu.VMEM((dofs, blocks, node_count, modes), jnp.float32),
            pltpu.VMEM((cols * blocks * sub, modes), jnp.float32),
            pltpu.SMEM(src_rows.shape, jnp.int32),
            pltpu.SMEM(dst_nodes.shape, jnp.int32),
            pltpu.SMEM(counts.shape, jnp.int32),
            pltpu.SMEM(spline_weights.shape, jnp.float32),
            dma((4,)),
            dma((stripes + 1,)),
            dma((cols * PARTS,)),
            dma,
            dma((cols - 1,)),
            dma,
            dma((cols - 1,)),
            dma,
            dma((cols - 1,)),
            dma,
            dma,
            dma,
            dma,
            dma,
            dma((3,)),
            dma((3,)),
            dma,
            dma,
            dma((3,)),
            dma((2 + cols,)),
            dma((2,)),
        ],
        compiler_params=pltpu.CompilerParams(
            collective_id=0, has_side_effects=True, vmem_limit_bytes=32 * 1024 * 1024
        ),
    )(*in_hbm)


def solution(mesh):
    placed = (
        P(("groups", "blk"), "col"),
        P(("groups", "col"), "blk", None),
        P(None, "blk", None),
        P("blk", "col", None, None),
        P("blk", "col", None, None),
        P("blk", "col", None),
        P("blk", "col", None, None, None),
    )

    def shards(*operands):
        aic, downwash, node_modes = operands[:3]
        blocks, cols = lax.axis_size("blk"), lax.axis_size("col")
        small = blocks * aic.shape[0] <= 2 * node_modes.shape[2]
        even = blocks == cols == 4 and cols % 2 == 0 and node_modes.shape[0] % 2 == 0 and aic.shape[0] % (8 * cols) == 0 and downwash.shape[1] % 512 == 0
        if small and even:
            return by_kernel(*operands)
        return by_rotation(*operands)

    return jax.shard_map(
        shards, mesh=mesh, in_specs=placed, out_specs=P("groups", None), check_vma=False
    )
```

```python
import functools

import jax
import jax.numpy as jnp
from jax import lax
from jax.experimental import pallas as pl
from jax.experimental.pallas import tpu as pltpu
from jax.sharding import PartitionSpec as P


HIGHEST = lax.Precision.HIGHEST
PARTS = 2
AHEAD = 3
SECOND_AT = 0
THIRD_AT = 3
OPENING = 2
LAST_AT = 6
LATE_FROM = 2
AFTER = {4: ((0, 0),), 6: ((0, 1),)}
TAIL = ((0, 2), (1, 0), (1, 1), (1, 2))
FINAL = ()
ODD_AHEAD = 2


def shifted(value, axis, steps):
    count = lax.axis_size(axis)
    pairs = [(source, (source + steps) % count) for source in range(count)]
    return lax.ppermute(value, axis, pairs)


def by_rotation(aic, downwash, node_modes, src_rows, dst_nodes, counts, spline_weights):
    cycle_size = lax.axis_size("blk")
    col_count = lax.axis_size("col")
    device = lax.axis_index("blk")
    own_block = downwash[0]
    panel_rows = own_block.shape[0]

    def product(shapes, source):
        columns = lax.dynamic_slice_in_dim(aic, source * panel_rows, panel_rows, 1)
        return jnp.dot(
            columns, shapes, precision=lax.Precision.HIGHEST, preferred_element_type=jnp.float32
        )

    halfway = cycle_size // 2

    def advance(offset, running):
        pressure, forward, behind = running
        forward = shifted(forward, "blk", 1)
        behind = shifted(behind, "blk", -1)
        pressure = pressure + product(forward, (device - offset) % cycle_size)
        pressure = pressure + product(behind, (device + offset) % cycle_size)
        return (pressure, forward, behind)

    pressure = product(own_block, device)
    pressure, forward, behind = lax.fori_loop(1, halfway, advance, (pressure, own_block, own_block))
    forward = shifted(forward, "blk", 1)
    pressure = pressure + product(forward, (device - halfway) % cycle_size)
    slots = src_rows.shape[-1]
    slot_index = jnp.arange(slots, dtype=jnp.int32)
    all_rows, all_nodes, all_counts = (
        lax.all_gather(src_rows, "col", axis=1, tiled=True),
        lax.all_gather(dst_nodes, "col", axis=1, tiled=True),
        lax.all_gather(counts, "col", axis=1, tiled=True),
    )
    weight_all = lax.all_gather(spline_weights, "col", axis=1, tiled=True)
    sub_rows = pressure.shape[0] // col_count
    offsets = jnp.arange(col_count, dtype=jnp.int32)[:, None, None] * sub_rows
    shifted_rows = all_rows[0] + offsets
    row_ids = jnp.transpose(shifted_rows, (1, 0, 2)).reshape(cycle_size, col_count * slots)
    node_ids = jnp.transpose(all_nodes[0], (1, 0, 2)).reshape(cycle_size, col_count * slots)
    live_sub = (slot_index[None, None, :] < all_counts[0][:, :, None]).astype(jnp.float32)
    live = jnp.transpose(live_sub, (1, 0, 2)).reshape(cycle_size, col_count * slots)
    weight_rows = jnp.transpose(weight_all[0], (1, 2, 0, 3)).reshape(
        6, cycle_size, col_count * slots
    )
    node_count = node_modes.shape[1]
    forces = pressure[row_ids.T]
    picks = (node_ids[None, :, :] == jnp.arange(node_count, dtype=jnp.int32)[:, None, None]).astype(
        jnp.float32
    )
    spread = weight_rows[:, None, :, :] * live[None, None, :, :] * picks[None, :, :, :]
    spread = spread.reshape(6 * node_count, cycle_size, row_ids.shape[1])
    arrived_forces, arrived_spread = (
        lax.all_to_all(forces, "blk", split_axis=1, concat_axis=1, tiled=True),
        lax.all_to_all(spread, "blk", split_axis=1, concat_axis=1, tiled=True),
    )
    loads = jnp.einsum(
        "jsc,csk->jk", arrived_spread, arrived_forces, precision=lax.Precision.HIGHEST
    )
    flat_modes = node_modes.reshape(6 * node_count, node_modes.shape[2])
    modal = jnp.einsum("jm,jk->mk", flat_modes, loads, precision=lax.Precision.HIGHEST)
    return lax.psum(modal, ("blk", "col"))


def split(value):
    high = value.astype(jnp.bfloat16)
    low = (value - high.astype(jnp.float32)).astype(jnp.bfloat16)
    return high, low


def exchange_kernel(
    blocks,
    cols,
    aic,
    panels,
    node_modes,
    rows_hbm,
    nodes_hbm,
    counts_hbm,
    weights_hbm,
    out,
    influence,
    shapes,
    shapes_high,
    shapes_low,
    partial,
    half_in,
    half_out,
    cross_in,
    gather_in,
    pressure,
    spline,
    mode_rows,
    force,
    rows_list,
    nodes_list,
    counts,
    weights,
    list_sem,
    panel_sem,
    aic_recv,
    aic_send,
    half_recv,
    half_send,
    cross_recv,
    cross_send,
    final_recv,
    final_send,
    gather_recv,
    gather_send,
    cast_recv,
    cast_send,
    chain_recv,
    chain_send,
    spline_recv,
    spline_send,
    mode_recv,
    mode_send,
    mode_plane_recv,
):
    b = lax.axis_index("blk")
    c = lax.axis_index("col")
    chunks, _, sub, depth = influence.shape
    dofs, _, node_count, modes = mode_rows.shape
    owners, slots = rows_list.shape[2:]
    width = panels.shape[2]
    last = chunks - 1
    early = range(last)
    parts = PARTS
    span = depth // parts
    total_pieces = chunks * parts
    middle = blocks // 2
    length = dofs * owners * node_count

    def on_line(k):
        return lax.rem(b + k, blocks)

    def on_plane(k):
        return lax.rem(c + k, cols)

    def far_target(j):
        falling = blocks - 1 - j
        rising = j
        falling = jnp.where(falling <= b, falling - 1, falling)
        rising = jnp.where(rising >= b, rising + 1, rising)
        return jnp.where(b < middle, falling, rising)

    def remote(where, source, target, send, recv):
        return pltpu.make_async_remote_copy(
            src_ref=source,
            dst_ref=target,
            send_sem=send,
            recv_sem=recv,
            device_id=where,
            device_id_type=pl.DeviceIdType.MESH,
        )

    def settle(ref, sem):
        pltpu.make_async_copy(ref, ref, sem).wait()

    barrier = pltpu.get_barrier_semaphore()
    for z in range(blocks):
        for x in range(cols):
            if (z == 0) != (x == 0):
                pl.semaphore_signal(
                    barrier,
                    inc=1,
                    device_id={"blk": on_line(z), "col": on_plane(x)},
                    device_id_type=pl.DeviceIdType.MESH,
                )

    list_copies = []
    lists = ((rows_hbm, rows_list), (nodes_hbm, nodes_list), (counts_hbm, counts), (weights_hbm, weights))
    for i, (source, target) in enumerate(lists):
        list_copies.append(pltpu.make_async_copy(source, target, list_sem.at[i]))
        list_copies[-1].start()
    stripes = panel_sem.shape[0] - 1
    stripe = depth // stripes
    panel_copies = []
    for p in range(stripes):
        where = pl.ds(p * stripe, stripe)
        panel_copies.append(
            pltpu.make_async_copy(panels.at[0, where], shapes.at[where], panel_sem.at[p])
        )
        panel_copies[-1].start()

    def piece_of(index):
        q, h = divmod(index, parts)
        return q, pl.ds(h * span, span)

    def aic_piece(index, peer):
        q, h = divmod(index, parts)
        start = pl.multiple_of(peer * depth + h * span, 128)
        return aic.at[pl.ds(q * sub, sub), pl.ds(start, span)]

    for index in range(total_pieces):
        q, where = piece_of(index)
        pltpu.make_async_copy(
            aic_piece(index, b), influence.at[q, b, :, where], aic_recv.at[index]
        ).start()
    half = cols // 2
    share = dofs // 2
    dof_span = pl.ds((c // half) * share, share)
    sends_modes = lax.rem(c, half) == half - 1
    own_modes = pltpu.make_async_copy(
        node_modes.at[dof_span], mode_rows.at[dof_span, b], panel_sem.at[stripes]
    )

    @pl.when(sends_modes)
    def _():
        own_modes.start()

    pl.semaphore_wait(barrier, blocks + cols - 2)

    def send_piece(index, parity):
        if index >= total_pieces:
            return
        q, where = piece_of(index)

        @pl.when(lax.rem(c, 2) == parity)
        def _():
            for j in range(blocks - 1):
                peer = far_target(j)
                remote(
                    {"blk": peer},
                    aic_piece(index, peer),
                    influence.at[q, b, :, where],
                    aic_send,
                    aic_recv.at[index],
                ).start()

    def await_piece(index):
        q, where = piece_of(index)
        settle(influence.at[q, :, :, where], aic_recv.at[index])
        send_piece(index + AHEAD, 0)
        send_piece(index + ODD_AHEAD, 1)

    own = jnp.where(b < middle, 0, middle)
    own_pair = pl.ds(own, middle)
    other_pair = pl.ds(middle - own, middle)
    near = 2 * own + 1 - b
    inward = jnp.where(b < middle, middle - 1, middle)
    team = middle * cols
    place = (b - own) * cols + c
    across = blocks - 1 - b
    inner = jnp.logical_and(b >= middle - 1, b <= middle)

    def chain(stage, peer, blocks_of):
        remote(
            {"blk": peer},
            spline.at[c, blocks_of],
            spline.at[c, blocks_of],
            chain_send.at[stage],
            chain_recv.at[stage],
        ).start()

    def mode_chain(stage, peer, blocks_of):
        remote(
            {"blk": peer},
            mode_rows.at[dof_span, blocks_of],
            mode_rows.at[dof_span, blocks_of],
            mode_send.at[stage],
            mode_recv.at[stage],
        ).start()

    def await_chain(stage, count):
        settle(spline.at[c, pl.ds(0, count)], chain_recv.at[stage])

        @pl.when(sends_modes)
        def _():
            settle(mode_rows.at[dof_span, pl.ds(0, count)], mode_recv.at[stage])

    def first_stage_modes():
        @pl.when(sends_modes)
        def _():
            remote(
                {"blk": near},
                node_modes.at[dof_span],
                mode_rows.at[dof_span, b],
                mode_send.at[0],
                mode_recv.at[0],
            ).start()

    def second_stage():
        await_chain(0, 1)

        @pl.when(sends_modes)
        def _():
            own_modes.wait()

        @pl.when(inner)
        def _():
            chain(1, across, own_pair)

            @pl.when(sends_modes)
            def _():
                mode_chain(1, across, own_pair)

    def third_stage():
        @pl.when(inner)
        def _():
            await_chain(1, middle)
            chain(2, near, other_pair)

            @pl.when(sends_modes)
            def _():
                mode_chain(2, near, other_pair)

            share_lists()

    def last_stage():
        @pl.when(jnp.logical_not(inner))
        def _():
            await_chain(2, middle)
            share_lists()

    def share_lists():
        for k in range(1, cols):
            remote(
                {"col": on_plane(k)},
                spline.at[c],
                spline.at[c],
                spline_send,
                spline_recv,
            ).start()

        @pl.when(sends_modes)
        def _():
            for k in range(1, cols):
                remote(
                    {"col": on_plane(k)},
                    mode_rows.at[dof_span],
                    mode_rows.at[dof_span],
                    mode_send.at[2 + k],
                    mode_plane_recv.at[c // half],
                ).start()

    first_stage_modes()
    for index in range(OPENING):
        send_piece(index, 0)
        send_piece(index, 1)

    row_at = lax.broadcasted_iota(jnp.int32, (sub, length), 0)
    column_at = lax.broadcasted_iota(jnp.int32, (sub, length), 1)
    total = jnp.zeros((sub, length), jnp.float32)
    for copy in list_copies:
        copy.wait()
    for o in range(owners):
        for s in range(slots):
            live = s < counts[0, 0, o]
            row = jnp.where(live, rows_list[0, 0, o, s], -1)
            node = nodes_list[0, 0, o, s] + o * node_count
            spread = jnp.zeros((sub, length), jnp.float32)
            for d in range(dofs):
                spread = jnp.where(
                    column_at == node + d * owners * node_count,
                    weights[0, 0, d, o, s],
                    spread,
                )
            total = total + jnp.where(row_at == row, spread, 0.0)
    spline[c, b] = total
    remote(
        {"blk": near}, spline.at[c, b], spline.at[c, b], chain_send.at[0], chain_recv.at[0]
    ).start()
    for index in range(OPENING, max(AHEAD, ODD_AHEAD)):
        if index < AHEAD:
            send_piece(index, 0)
        if index < ODD_AHEAD:
            send_piece(index, 1)

    for p in range(stripes):
        panel_copies[p].wait()
        where = pl.ds(p * stripe, stripe)
        high, low = split(shapes[where])
        shapes_high[where] = high
        shapes_low[where] = low

    def multiply(q, start, stop):
        where = pl.ds(start * span, (stop - start) * span)
        lines = blocks * sub
        high, low = split(influence[q, :, :, where].reshape(lines, (stop - start) * span))
        product = jnp.dot(
            jnp.concatenate([high, low], axis=0),
            shapes_high[where],
            preferred_element_type=jnp.float32,
        )
        rest = jnp.dot(high, shapes_low[where], preferred_element_type=jnp.float32)
        return product[:lines] + (product[lines:] + rest)

    def to_half(q):
        partial[q] = multiply(q, 0, parts).reshape(blocks, sub, width)
        for r in range(cols):

            @pl.when(jnp.logical_or(b != inward, c != r))
            def _():
                remote(
                    {"blk": inward, "col": r},
                    partial.at[q, r],
                    half_in.at[q, place],
                    half_send,
                    half_recv.at[q],
                ).start()

        @pl.when(inner)
        def _():
            half_in[q, place] = partial[q, c]

    def half_sum(q):
        @pl.when(inner)
        def _():
            settle(half_in.at[q, pl.ds(0, team - 1)], half_recv.at[q])
            total = half_in[q, 0]
            for source in range(1, team):
                total = total + half_in[q, source]
            half_out[q] = total
            remote(
                {"blk": across}, half_out.at[q], cross_in.at[q], cross_send, cross_recv.at[q]
            ).start()

    def full_sum(q):
        @pl.when(inner)
        def _():
            settle(cross_in.at[q], cross_recv.at[q])
            pressure[q, c] = half_out[q] + cross_in[q]
            for peer in (near, b):
                for k in range(cols):
                    if peer is b and k == 0:
                        continue
                    remote(
                        {"blk": peer, "col": on_plane(k)},
                        pressure.at[q, c],
                        pressure.at[q, c],
                        final_send,
                        final_recv.at[q],
                    ).start()

    def await_final(q):
        @pl.when(inner)
        def _():
            settle(pressure.at[q, pl.ds(0, cols - 1)], final_recv.at[q])

        @pl.when(jnp.logical_not(inner))
        def _():
            settle(pressure.at[q], final_recv.at[q])

    def seat(r):
        return middle - 1 + r % 2

    def chair(r):
        return r // 2 * 2 + 1

    is_owner = jnp.logical_and(inner, lax.rem(c, 2) == 1)
    mine = jnp.where(inner, c // 2 * 2 + b - (middle - 1), 0)

    def to_owners():
        for r in range(cols):

            @pl.when(jnp.logical_or(b != seat(r), c != chair(r)))
            def _():
                remote(
                    {"blk": seat(r), "col": chair(r)},
                    partial.at[last, r],
                    gather_in.at[b * cols + c],
                    gather_send,
                    gather_recv,
                ).start()

    def cast():
        @pl.when(is_owner)
        def _():
            gather_in[b * cols + c] = partial[last, mine]
            settle(gather_in.at[pl.ds(0, blocks * cols - 1)], gather_recv)
            total = gather_in[0]
            for source in range(1, blocks * cols):
                total = total + gather_in[source]
            pressure[last, mine] = total
            for j in range(blocks):
                for k in range(cols):
                    if j == blocks - 1 and k == 0:
                        continue
                    peer = b if j == blocks - 1 else far_target(j)
                    remote(
                        {"blk": peer, "col": on_plane(k)},
                        pressure.at[last, mine],
                        pressure.at[last, mine],
                        cast_send,
                        cast_recv,
                    ).start()

    def await_cast():
        @pl.when(is_owner)
        def _():
            settle(pressure.at[last, pl.ds(0, cols - 1)], cast_recv)

        @pl.when(jnp.logical_not(is_owner))
        def _():
            settle(pressure.at[last], cast_recv)

    def make_force():
        settle(spline.at[pl.ds(0, cols - 1)], spline_recv)
        for s in range(2):

            @pl.when(c != s * half + half - 1)
            def _():
                settle(mode_rows.at[pl.ds(s * share, share)], mode_plane_recv.at[s])

        force[...] = jnp.dot(
            spline[...].reshape(cols * blocks * sub, length),
            mode_rows[...].reshape(length, modes),
            precision=HIGHEST,
            preferred_element_type=jnp.float32,
        )

    def modal(start, stop):
        rows = (stop - start) * blocks * sub
        force_high, force_low = split(force[pl.ds(start * blocks * sub, rows)])
        high, low = split(pressure[start:stop].reshape(rows, width))
        return lax.dot_general(
            jnp.concatenate([force_high, force_high, force_low], axis=0),
            jnp.concatenate([high, low, high], axis=0),
            (((0,), (0,)), ((), ())),
            preferred_element_type=jnp.float32,
        )

    for index in range(total_pieces):
        await_piece(index)
        q, h = divmod(index, parts)
        if q == last:
            product = multiply(last, h, h + 1)
            ending = product if h == 0 else ending + product
        elif h == parts - 1:
            to_half(q)
        if index == SECOND_AT:
            second_stage()
        if index == THIRD_AT:
            third_stage()
        if index == LAST_AT:
            last_stage()
        for kind, q in AFTER.get(index, ()):
            (half_sum, full_sum)[kind](q)
    partial[last] = ending.reshape(blocks, sub, width)
    to_owners()
    if LAST_AT is None:
        last_stage()
    for kind, q in TAIL:
        (half_sum, full_sum)[kind](q)
    cast()
    for kind, q in FINAL:
        (half_sum, full_sum)[kind](q)
    make_force()
    for q in range(LATE_FROM):
        await_final(q)
    out[...] = modal(0, LATE_FROM)
    for q in range(LATE_FROM, last):
        await_final(q)
    await_cast()
    out[...] += modal(LATE_FROM, chunks)

    settle(influence.at[pl.ds(0, blocks - 1)], aic_send)
    settle(spline.at[c, 0], chain_send.at[0])

    @pl.when(inner)
    def _():
        settle(spline.at[c, pl.ds(0, middle)], chain_send.at[1])
        settle(spline.at[c, pl.ds(0, middle)], chain_send.at[2])

    settle(spline.at[pl.ds(0, cols - 1)], spline_send)
    @pl.when(inner)
    def _():
        settle(partial.at[pl.ds(0, last), pl.ds(0, cols - 1)], half_send)
        settle(half_out, cross_send)
        settle(half_in.at[:, pl.ds(0, team - 1)], final_send)

    @pl.when(jnp.logical_not(inner))
    def _():
        settle(partial.at[pl.ds(0, last)], half_send)

    @pl.when(is_owner)
    def _():
        settle(partial.at[last, pl.ds(0, cols - 1)], gather_send)
        settle(gather_in.at[pl.ds(0, blocks * cols - 1)], cast_send)

    @pl.when(jnp.logical_not(is_owner))
    def _():
        settle(partial.at[last], gather_send)

    @pl.when(sends_modes)
    def _():
        settle(mode_rows.at[dof_span, 0], mode_send.at[0])

        @pl.when(inner)
        def _():
            settle(mode_rows.at[dof_span, pl.ds(0, middle)], mode_send.at[1])
            settle(mode_rows.at[dof_span, pl.ds(0, middle)], mode_send.at[2])

        for k in range(1, cols):
            settle(mode_rows.at[dof_span], mode_send.at[2 + k])


def by_kernel(aic, downwash, node_modes, src_rows, dst_nodes, counts, spline_weights):
    blocks = lax.axis_size("blk")
    cols = lax.axis_size("col")
    rows = aic.shape[0]
    sub = rows // cols
    depth, width = downwash.shape[1:]
    dofs, node_count, modes = node_modes.shape
    length = dofs * blocks * node_count
    stripes = 4
    dma = pltpu.SemaphoreType.DMA
    anywhere = pl.BlockSpec(memory_space=pl.ANY)
    operands = (aic, downwash, node_modes, src_rows, dst_nodes, counts, spline_weights)
    in_hbm = [pltpu.with_memory_space_constraint(v, pltpu.MemorySpace.HBM) for v in operands]
    return pl.pallas_call(
        functools.partial(exchange_kernel, blocks, cols),
        name="gaf_exchange",
        out_shape=jax.ShapeDtypeStruct((modes, width), jnp.float32),
        in_specs=[anywhere] * 7,
        out_specs=pl.BlockSpec(memory_space=pltpu.VMEM),
        scratch_shapes=[
            pltpu.VMEM((cols, blocks, sub, depth), jnp.float32),
            pltpu.VMEM((depth, width), jnp.float32),
            pltpu.VMEM((depth, width), jnp.bfloat16),
            pltpu.VMEM((depth, width), jnp.bfloat16),
            pltpu.VMEM((cols, blocks, sub, width), jnp.float32),
            pltpu.VMEM((cols - 1, blocks // 2 * cols, sub, width), jnp.float32),
            pltpu.VMEM((cols - 1, sub, width), jnp.float32),
            pltpu.VMEM((cols - 1, sub, width), jnp.float32),
            pltpu.VMEM((blocks * cols, sub, width), jnp.float32),
            pltpu.VMEM((cols, blocks, sub, width), jnp.float32),
            pltpu.VMEM((cols, blocks, sub, length), jnp.float32),
            pltpu.VMEM((dofs, blocks, node_count, modes), jnp.float32),
            pltpu.VMEM((cols * blocks * sub, modes), jnp.float32),
            pltpu.SMEM(src_rows.shape, jnp.int32),
            pltpu.SMEM(dst_nodes.shape, jnp.int32),
            pltpu.SMEM(counts.shape, jnp.int32),
            pltpu.SMEM(spline_weights.shape, jnp.float32),
            dma((4,)),
            dma((stripes + 1,)),
            dma((cols * PARTS,)),
            dma,
            dma((cols - 1,)),
            dma,
            dma((cols - 1,)),
            dma,
            dma((cols - 1,)),
            dma,
            dma,
            dma,
            dma,
            dma,
            dma((3,)),
            dma((3,)),
            dma,
            dma,
            dma((3,)),
            dma((2 + cols,)),
            dma((2,)),
        ],
        compiler_params=pltpu.CompilerParams(
            collective_id=0, has_side_effects=True, vmem_limit_bytes=32 * 1024 * 1024
        ),
    )(*in_hbm)


def solution(mesh):
    placed = (
        P(("groups", "blk"), "col"),
        P(("groups", "col"), "blk", None),
        P(None, "blk", None),
        P("blk", "col", None, None),
        P("blk", "col", None, None),
        P("blk", "col", None),
        P("blk", "col", None, None, None),
    )

    def shards(*operands):
        aic, downwash, node_modes = operands[:3]
        blocks, cols = lax.axis_size("blk"), lax.axis_size("col")
        small = blocks * aic.shape[0] <= 2 * node_modes.shape[2]
        even = blocks == cols == 4 and cols % 2 == 0 and node_modes.shape[0] % 2 == 0 and aic.shape[0] % (8 * cols) == 0 and downwash.shape[1] % 512 == 0
        if small and even:
            return by_kernel(*operands)
        return by_rotation(*operands)

    return jax.shard_map(
        shards, mesh=mesh, in_specs=placed, out_specs=P("groups", None), check_vma=False
    )
```
